32 devices in a mesh: gx: 8 (over y, x, core), vert: 4 (over z).
Axes of the slice: x: 2, y: 2, z: 4, core: 2. Of those that a mesh axis runs over, the one named last changes fastest.
Arguments:
- distribution: float32 [2, 96, 96, 1024], P(None, 'vert', None, 'gx'), may hold values from 0 to 4, as said below
- wall_type: int32 [2, 64], P(None, 'gx'), may hold values from 0 to 2
- wall_temp_index: int32 [2, 64], P(None, 'gx'), may hold values from 0 to 1
- wall_temps: float32 [2], replicated, may hold values from 0.5 to 2
- accommodation: int32 [3], replicated, may hold values from 0 to 50
Outputs:
- advanced: float32 [2, 96, 96, 1024], P(None, 'vert', None, 'gx')
The draws below stay inside these ranges and needn't reach their ends.
Inputs may be any that keep to these rules, and one draw needn't show every extreme that they name: `distribution`: nonnegative phase-space densities.
All inputs are finite; a program needn't handle non-finite values.
Results may differ from the reference program's by a relative error of at most 0.0003.
Values sent between devices are 32-bit elements; how exact they have to be, the bound alone decides.
No kernel may reach another device: no remote copies, remote signals or barrier semaphores. Data moves between devices by JAX's collectives and lax.ppermute only.
A program may use at most 128 MiB of HBM per device.

```python
import math
import jax
import jax.numpy as jnp
from jax import lax

SPEED_NODES_HORIZ = 96
SPEED_NODES_VERT = 96
Y = 16
ITERS = 4
NTEMP = 2
NTYPE = 3
NX = 64
GRID_SITE_COUNT = 1024
BAND = 24
N_VERT = 4


def draw_distribution(key, part):
    stochastic_seeds = jax.random.split(key, 8)
    particle_concentration = jnp.exp(jax.random.uniform(stochastic_seeds[0], (GRID_SITE_COUNT,), jnp.float32, math.log(0.5), math.log(2.0)))
    thermal_level = jnp.exp(jax.random.uniform(stochastic_seeds[1], (GRID_SITE_COUNT,), jnp.float32, math.log(0.6), math.log(1.6)))
    bulk_flow_horizontal = jax.random.uniform(stochastic_seeds[2], (GRID_SITE_COUNT,), jnp.float32, -0.3, 0.3)
    bulk_flow_vertical = jax.random.uniform(stochastic_seeds[3], (GRID_SITE_COUNT,), jnp.float32, -0.3, 0.3)
    speed_x = 4.5 * (2.0 * jnp.arange(SPEED_NODES_HORIZ, dtype=jnp.float32) + 1.0 - SPEED_NODES_HORIZ) / SPEED_NODES_HORIZ
    rows = jnp.arange(SPEED_NODES_VERT, dtype=jnp.int32)
    band_rows = SPEED_NODES_VERT // N_VERT
    band_index = rows // band_rows
    lower = band_index // 2 * band_rows + rows % band_rows
    velocity = jnp.where(band_index % 2 == 0, lower, SPEED_NODES_VERT - 1 - lower)
    speed_y = 4.5 * (2.0 * velocity.astype(jnp.float32) + 1.0 - SPEED_NODES_VERT) / SPEED_NODES_VERT
    relative_speed_horizontal = speed_x[None, :, None] - bulk_flow_horizontal
    relative_speed_vertical = speed_y[:, None, None] - bulk_flow_vertical
    gaussian_distribution = particle_concentration / (math.pi * thermal_level) * jnp.exp(-(relative_speed_horizontal * relative_speed_horizontal + relative_speed_vertical * relative_speed_vertical) / thermal_level)
    shape = (SPEED_NODES_VERT, SPEED_NODES_HORIZ, GRID_SITE_COUNT)
    linear_integral_term = gaussian_distribution * jax.random.uniform(stochastic_seeds[4], shape, jnp.float32, 0.7, 1.3)
    quadratic_integral_term = 0.5 * thermal_level * linear_integral_term * jax.random.uniform(stochastic_seeds[5], shape, jnp.float32, 0.7, 1.3)
    linear_integral_term = linear_integral_term + 0.01 * jax.random.uniform(stochastic_seeds[6], shape, jnp.float32, 0.5, 1.5)
    quadratic_integral_term = quadratic_integral_term + 0.01 * jax.random.uniform(stochastic_seeds[7], shape, jnp.float32, 0.5, 1.5)
    return jnp.stack([linear_integral_term, quadratic_integral_term]).astype(jnp.float32)


def with_ends(values, key, low, largest):
    longest = values.shape.index(max(values.shape))
    spots = []
    for shift in (0, 1):
        where = [jax.random.randint(jax.random.fold_in(key, axis), (), 0, length) for axis, length in enumerate(values.shape)]
        where[longest] = (where[longest] + shift) % values.shape[longest]
        spots.append(tuple(where))
    return values.at[spots[0]].set(low).at[spots[1]].set(largest)


def setup_inputs(seed: int = 0) -> dict:
    streams_of = jax.random.split(jax.random.key(seed), 6)
    return {
        "distribution": draw_distribution(jax.random.fold_in(streams_of[5], 71), 0),
        "wall_type": with_ends(jax.random.randint(streams_of[1], (2, NX), 0, NTYPE), jax.random.fold_in(streams_of[1], 1), 0, NTYPE - 1).astype(jnp.int32),
        "wall_temp_index": with_ends(jax.random.randint(streams_of[2], (2, NX), 0, NTEMP), jax.random.fold_in(streams_of[2], 1), 0, NTEMP - 1).astype(jnp.int32),
        "wall_temps": jnp.clip(jnp.exp(jax.random.uniform(streams_of[3], (NTEMP,), jnp.float32, math.log(0.5), math.log(2.0))), 0.5, 2.0),
        "accommodation": jax.random.randint(streams_of[4], (NTYPE,), 0, 51).astype(jnp.int32),
    }


vmax_speed = 4.5
courant = 0.5
diffusivity_ratio = 2.0 / 3.0
relaxation_multiplier = 2.5
shear_exponent = 0.19
time_increment = courant / vmax_speed
highest = lax.Precision.HIGHEST


def speeds(number):
    return vmax_speed * (2.0 * jnp.arange(number, dtype=jnp.float32) + 1.0 - number) / number


def folded_speeds():
    rows = jnp.arange(SPEED_NODES_VERT, dtype=jnp.int32)
    band_index = rows // BAND
    offset = rows % BAND
    lower = (band_index // 2) * BAND + offset
    velocity = jnp.where(band_index % 2 == 0, lower, SPEED_NODES_VERT - 1 - lower)
    return vmax_speed * (2.0 * velocity.astype(jnp.float32) + 1.0 - SPEED_NODES_VERT) / SPEED_NODES_VERT


def mirror_rows(values):
    shape = values.shape
    paired = values.reshape((shape[0], N_VERT // 2, 2, BAND) + shape[2:])
    return jnp.flip(paired, axis=2).reshape(shape)


def cell_weight():
    return (2.0 * vmax_speed / SPEED_NODES_HORIZ) * (2.0 * vmax_speed / SPEED_NODES_VERT)


def shift_flat(values, offset):
    extent = abs(offset)
    padding = jnp.zeros(values.shape[:-1] + (extent,), values.dtype)
    if offset > 0:
        return jnp.concatenate([padding, values[..., :-extent]], axis=-1)
    return jnp.concatenate([values[..., extent:], padding], axis=-1)


def beam_term(center, linear_integral_term, quadratic_integral_term, number):
    return -0.5 * number * (3.0 * center - 4.0 * linear_integral_term + quadratic_integral_term) + 0.5 * number * number * (center - 2.0 * linear_integral_term + quadratic_integral_term)


def shakhov_target(speed_x, speed_y, macroscopic_quantities):
    particle_concentration, bulk_flow_horizontal, bulk_flow_vertical, thermal_level, thermal_current_horizontal, thermal_current_vertical = macroscopic_quantities
    relative_speed_horizontal = speed_x[None, :, None] - bulk_flow_horizontal
    relative_speed_vertical = speed_y[:, None, None] - bulk_flow_vertical
    kinetic_content_sum = (relative_speed_horizontal * relative_speed_horizontal + relative_speed_vertical * relative_speed_vertical) / thermal_level
    relaxed_distribution_target = particle_concentration / (math.pi * thermal_level) * jnp.exp(-kinetic_content_sum)
    multiplier_coefficient = (1.0 - diffusivity_ratio) * 0.8 * (relative_speed_horizontal * thermal_current_horizontal + relative_speed_vertical * thermal_current_vertical) / (particle_concentration * thermal_level * thermal_level)
    linear_integral_term = relaxed_distribution_target * (1.0 + multiplier_coefficient * (kinetic_content_sum - 2.0))
    quadratic_integral_term = 0.5 * thermal_level * relaxed_distribution_target * (1.0 + multiplier_coefficient * (kinetic_content_sum - 1.0))
    return jnp.stack([linear_integral_term, quadratic_integral_term])


def advance(state, ghosts, neighbours, speed_x, speed_y, macroscopic_quantities):
    lower_one, lower_two, upper_one, upper_two = ghosts
    left_two, left_one, right_one, right_two = neighbours
    total = state.shape[-1]
    row_pos = jnp.arange(total, dtype=jnp.int32) % Y

    def spread(ghost):
        return jnp.repeat(ghost, Y, axis=-1)

    down_one = jnp.where(row_pos >= 1, shift_flat(state, 1), spread(lower_one))
    down_two = jnp.where(row_pos >= 2, shift_flat(state, 2), jnp.where(row_pos == 1, spread(lower_one), spread(lower_two)))
    up_one = jnp.where(row_pos <= Y - 2, shift_flat(state, -1), spread(upper_one))
    up_two = jnp.where(row_pos <= Y - 3, shift_flat(state, -2), jnp.where(row_pos == Y - 2, spread(upper_one), spread(upper_two)))
    along_x = speed_x[None, None, :, None]
    along_y = speed_y[None, :, None, None]
    first_x = jnp.where(along_x > 0, left_one, right_one)
    second_x = jnp.where(along_x > 0, left_two, right_two)
    first_y = jnp.where(along_y > 0, down_one, up_one)
    second_y = jnp.where(along_y > 0, down_two, up_two)
    particle_concentration = macroscopic_quantities[0]
    thermal_level = macroscopic_quantities[3]
    relaxation_frequency = time_increment * relaxation_multiplier * particle_concentration * jnp.power(thermal_level, shear_exponent)
    target = shakhov_target(speed_x, speed_y, macroscopic_quantities)
    moved = state + beam_term(state, first_x, second_x, jnp.abs(along_x) * time_increment)
    moved = moved + beam_term(state, first_y, second_y, jnp.abs(along_y) * time_increment)
    return moved + relaxation_frequency * (target - state)


def wall_tables(wall_type, wall_temp_index, wall_temps, accommodation):
    type_hits = wall_type[..., None] == jnp.arange(NTYPE, dtype=jnp.int32)
    alpha = jnp.sum(jnp.where(type_hits, accommodation.astype(jnp.float32), 0.0), axis=-1) / 100.0
    temp_hits = wall_temp_index[..., None] == jnp.arange(NTEMP, dtype=jnp.int32)
    wall_heat = jnp.sum(jnp.where(temp_hits, wall_temps, 0.0), axis=-1)
    grid_x = speeds(SPEED_NODES_HORIZ)
    grid_y = speeds(SPEED_NODES_VERT)
    kinetic_content_sum = grid_y[:, None] * grid_y[:, None] + grid_x[None, :] * grid_x[None, :]
    temps = wall_temps[:, None, None]
    flux_in = cell_weight() * jnp.sum(jnp.maximum(grid_y, 0.0)[None, :, None] * jnp.exp(-kinetic_content_sum[None] / temps) / (math.pi * temps), axis=(1, 2))
    denom = jnp.sum(jnp.where(temp_hits, flux_in, 0.0), axis=-1)
    return alpha, wall_heat, denom


def wall_ghost(alpha, wall_heat, wall_density, mirrored, speed_x, speed_y):
    kinetic_content_sum = speed_y[:, None, None] * speed_y[:, None, None] + speed_x[None, :, None] * speed_x[None, :, None]
    gaussian_distribution = jnp.exp(-kinetic_content_sum / wall_heat) / (math.pi * wall_heat)
    diffuse = jnp.stack([wall_density * gaussian_distribution, 0.5 * wall_heat * wall_density * gaussian_distribution])
    return alpha * diffuse + (1.0 - alpha) * mirrored


def wall_flux(dens_g, speed_y):
    bottom = jnp.sum(jnp.maximum(-speed_y, 0.0)[:, None, None] * dens_g[..., 0::Y], axis=(0, 1))
    top = jnp.sum(jnp.maximum(speed_y, 0.0)[:, None, None] * dens_g[..., Y - 1::Y], axis=(0, 1))
    return cell_weight() * jnp.stack([bottom, top])


def conserved_moments(state, speed_x, speed_y):
    grid_x = jnp.broadcast_to(speed_x[None, :], (speed_y.shape[0], speed_x.shape[0]))
    grid_y = jnp.broadcast_to(speed_y[:, None], grid_x.shape)
    ones = jnp.ones_like(grid_x)
    zeros = jnp.zeros_like(grid_x)
    basis_g = jnp.stack([ones, grid_x, grid_y, grid_x * grid_x + grid_y * grid_y])
    basis_h = jnp.stack([zeros, zeros, zeros, ones])
    part_g = jnp.einsum('kji,jic->kc', basis_g, state[0], precision=highest)
    part_h = jnp.einsum('kji,jic->kc', basis_h, state[1], precision=highest)
    return cell_weight() * (part_g + part_h)


def macro_fields(invariant_quantities, thermal_current_pair):
    particle_concentration = invariant_quantities[0]
    bulk_flow_horizontal = invariant_quantities[1] / particle_concentration
    bulk_flow_vertical = invariant_quantities[2] / particle_concentration
    thermal_level = (2.0 / 3.0) * (invariant_quantities[3] / particle_concentration - bulk_flow_horizontal * bulk_flow_horizontal - bulk_flow_vertical * bulk_flow_vertical)
    return (particle_concentration, bulk_flow_horizontal, bulk_flow_vertical, thermal_level, thermal_current_pair[0], thermal_current_pair[1])


def centered_heat(state, speed_x, speed_y, bulk_flow_horizontal, bulk_flow_vertical):
    def accumulate(total, items):
        dens_row, extra_row, speed_row = items
        relative_speed_horizontal = speed_x[:, None] - bulk_flow_horizontal
        relative_speed_vertical = speed_row - bulk_flow_vertical
        kinetic_content_sum = (relative_speed_horizontal * relative_speed_horizontal + relative_speed_vertical * relative_speed_vertical) * dens_row + extra_row
        return total + jnp.stack([jnp.sum(relative_speed_horizontal * kinetic_content_sum, axis=0), jnp.sum(relative_speed_vertical * kinetic_content_sum, axis=0)]), None

    start = jnp.zeros((2, state.shape[-1]), jnp.float32)
    total, unused = lax.scan(accumulate, start, (state[0], state[1], speed_y))
    return cell_weight() * total


def reference(distribution, wall_type, wall_temp_index, wall_temps, accommodation):
    speed_x = speeds(SPEED_NODES_HORIZ)
    speed_y = folded_speeds()
    alpha, wall_heat, denom = wall_tables(wall_type, wall_temp_index, wall_temps, accommodation)
    state = distribution
    for iteration in range(ITERS):
        invariant_quantities = conserved_moments(state, speed_x, speed_y)
        thermal_current_pair = centered_heat(state, speed_x, speed_y, invariant_quantities[1] / invariant_quantities[0], invariant_quantities[2] / invariant_quantities[0])
        macroscopic_quantities = macro_fields(invariant_quantities, thermal_current_pair)
        wall_density = wall_flux(state[0], speed_y) / denom
        mirror_b0 = mirror_rows(state[..., 0::Y])
        mirror_b1 = mirror_rows(state[..., 1::Y])
        mirror_t0 = mirror_rows(state[..., Y - 1::Y])
        mirror_t1 = mirror_rows(state[..., Y - 2::Y])
        lower_one = wall_ghost(alpha[0], wall_heat[0], wall_density[0], mirror_b0, speed_x, speed_y)
        lower_two = wall_ghost(alpha[0], wall_heat[0], wall_density[0], mirror_b1, speed_x, speed_y)
        upper_one = wall_ghost(alpha[1], wall_heat[1], wall_density[1], mirror_t0, speed_x, speed_y)
        upper_two = wall_ghost(alpha[1], wall_heat[1], wall_density[1], mirror_t1, speed_x, speed_y)

        def one_row(items):
            row_state, ghost_a, ghost_b, ghost_c, ghost_d, speed_row = items
            block = row_state[:, None]
            neighbours = (jnp.roll(block, 2 * Y, axis=-1), jnp.roll(block, Y, axis=-1), jnp.roll(block, -Y, axis=-1), jnp.roll(block, -2 * Y, axis=-1))
            ghost_rows = (ghost_a[:, None], ghost_b[:, None], ghost_c[:, None], ghost_d[:, None])
            return advance(block, ghost_rows, neighbours, speed_x, jnp.reshape(speed_row, (1,)), macroscopic_quantities)[:, 0]

        moved = lax.map(one_row, (jnp.moveaxis(state, 1, 0), jnp.moveaxis(lower_one, 1, 0), jnp.moveaxis(lower_two, 1, 0), jnp.moveaxis(upper_one, 1, 0), jnp.moveaxis(upper_two, 1, 0), speed_y))
        state = jnp.moveaxis(moved, 0, 1)
    return state
```

```python
import functools
import math

import jax
import jax.numpy as jnp
from jax import lax
from jax.experimental import pallas as pl
from jax.experimental.pallas import tpu as pltpu
from jax.sharding import PartitionSpec as P


Y = 16
ITERS = 4
NTEMP = 2
NTYPE = 3
SUB = 8
ROWS = 16

vmax_speed = 4.5
courant = 0.5
diffusivity_ratio = 2.0 / 3.0
relaxation_multiplier = 2.5
shear_exponent = 0.19
time_increment = courant / vmax_speed


class Sizes:
    def __init__(self, band, nx, cells, vert):
        self.band, self.nx, self.cells, self.vert = band, nx, cells, vert
        self.nv = band * vert
        self.groups = nx // SUB
        self.half = self.groups // 2
        self.wall_packs = -(-band // SUB)
        self.side_slots = cells // (2 * Y)
        self.side_packs = -(-band // self.side_slots)
        self.weight = 2.0 * vmax_speed / nx * (2.0 * vmax_speed / self.nv)

    def mirror_index(self, f, group, pack):
        return f * self.groups * self.wall_packs + group * self.wall_packs + pack

    @property
    def mirror_blocks(self):
        return 2 * self.groups * self.wall_packs


def lanes(sz):
    return lax.broadcasted_iota(jnp.int32, (1, sz.cells), 1)


def node_speed(index, number):
    return vmax_speed * (2.0 * index.astype(jnp.float32) + 1.0 - number) / number


def row_speed(sz, vert_index, offset):
    lower = vert_index // 2 * sz.band + offset
    return node_speed(jnp.where(vert_index % 2 == 0, lower, sz.nv - 1 - lower), sz.nv)


def beam_weights(speed):
    s = jnp.abs(speed) * time_increment
    return -1.5 * s + 0.5 * s * s, 2.0 * s - s * s, -0.5 * s + 0.5 * s * s


class Edges:
    def __init__(self, sz, parity):
        cells = sz.cells
        y = lanes(sz) % Y
        y = jnp.broadcast_to(y, (SUB, cells))
        even = parity == 0
        self.pair = y // 2
        self.odd_lane = y % 2
        first = jnp.where(even, 0, Y - 1)
        second = jnp.where(even, 1, Y - 2)
        self.one = y == first
        self.two = self.one | (y == second)
        self.shift_one = jnp.where(even, cells - 1, 1)
        self.shift_two = jnp.where(even, cells - 2, 2)
        self.unpack = jnp.where(even, Y, cells - 2)
        self.pack = jnp.where(even, 0, cells - (Y - 2))
        self.cells = cells

    def unpack_shift(self, slot):
        return lax.rem(self.unpack + (self.cells - 2 * slot), self.cells)

    def pack_shift(self, slot):
        return lax.rem(self.pack + 2 * slot, self.cells)


def roll(value, shift):
    if isinstance(shift, int) and shift == 0:
        return value
    return pltpu.roll(value, shift, 1)


class Packer:
    def __init__(self, sz, edges, right):
        self.sz, self.edges, self.right = sz, edges, right
        self.wall = self.side = None
        lane = lax.broadcasted_iota(jnp.int32, (SUB, sz.cells), 1)
        self.side_slot = lane // (2 * Y)

    def add(self, value, k):
        sz = self.sz
        slot = k % SUB
        moved = roll(value, self.edges.pack_shift(slot))
        self.wall = moved if slot == 0 else jnp.where(self.edges.pair == slot, moved, self.wall)
        slot = k % sz.side_slots
        shift = 2 * Y * slot
        if self.right:
            shift = (shift + 2 * Y) % sz.cells
        moved = roll(value, shift % sz.cells)
        self.side = moved if slot == 0 else jnp.where(self.side_slot == slot, moved, self.side)


def put_moments(sz, vert_index, sums, packet_ref, mirror_ref):
    (n, mx, my, pxx, pxy, pyy, extra, tx, ty) = [
        jnp.sum(part, axis=0, keepdims=True) * sz.weight for part in sums
    ]
    even = vert_index % 2 == 0
    zero = jnp.zeros_like(n)
    rows = [n, mx, my, pxx + pyy + extra, pxx, pxy, pyy, tx, ty]
    rows += [jnp.where(even, -my, zero), jnp.where(even, zero, my)]
    rows += [zero] * (ROWS - len(rows))
    for r, row in enumerate(rows):
        packet_ref[r : r + 1, :] = row
        mirror_ref[sz.mirror_blocks + r // SUB, r % SUB : r % SUB + 1, :] = row


class Moments:
    def __init__(self, shape):
        zero = jnp.zeros(shape, jnp.float32)
        self.g = [zero] * 4
        self.h = [zero] * 2

    def add(self, g, h):
        for sums, item in ((self.g, g), (self.h, h)):
            for order in range(len(sums)):
                item = sums[order] + item
                sums[order] = item

    def finish(self, sz, vert_index, speed_x, totals):
        s0, s1, s2, s3 = self.g
        m1, m2, m3 = s1, 2.0 * s2 - s1, 6.0 * (s3 - s2) + s1
        first = row_speed(sz, vert_index, jnp.zeros((1, 1), jnp.int32))
        last = row_speed(sz, vert_index, jnp.full((1, 1), sz.band, jnp.int32))
        b = jnp.broadcast_to(last, s0.shape)
        d = (last - first) / sz.band
        d = jnp.broadcast_to(d, s0.shape)
        t0 = s0
        t1 = b * s0 - d * m1
        t2 = b * (b * s0 - 2.0 * d * m1) + d * d * m2
        t3 = b * (b * (b * s0 - 3.0 * d * m1) + 3.0 * d * d * m2) - d * d * d * m3
        u0, su1 = self.h
        u1 = b * u0 - d * su1
        x2 = speed_x * speed_x
        new = (
            t0,
            speed_x * t0,
            t1,
            x2 * t0,
            speed_x * t1,
            t2,
            u0,
            speed_x * (x2 * t0 + t2 + u0),
            x2 * t1 + t3 + u1,
        )
        return tuple(a + c for a, c in zip(totals, new))


def zero_totals(sz):
    return tuple(jnp.zeros((SUB, sz.cells), jnp.float32) for _ in range(9))


def wall_rows(sz, face, type_ref, index_ref, temps_ref, acc_ref, wall_ref):
    lane = lanes(sz)
    column = lane // Y
    kind = jnp.zeros_like(lane)
    entry = jnp.zeros_like(lane)
    for x in range(sz.cells // Y):
        kind = jnp.where(column == x, type_ref[face, x], kind)
        entry = jnp.where(column == x, index_ref[face, x], entry)
    percent = jnp.zeros_like(lane)
    for t in range(NTYPE):
        percent = jnp.where(kind == t, acc_ref[t], percent)
    alpha = percent.astype(jnp.float32) / 100.0
    heat = jnp.ones((1, sz.cells), jnp.float32)
    denom = jnp.ones((1, sz.cells), jnp.float32)

    def grid(number):
        index = lax.broadcasted_iota(jnp.int32, (1, -(-number // 128) * 128), 1)
        return node_speed(index, number), index < number

    vx, in_x = grid(sz.nx)
    vy, in_y = grid(sz.nv)
    for t in range(NTEMP):
        temp = jnp.full((1, 1), temps_ref[t], jnp.float32)
        along = jnp.sum(jnp.where(in_x, jnp.exp(-vx * vx / temp), 0.0), axis=1, keepdims=True)
        across = jnp.sum(
            jnp.where(in_y, jnp.maximum(vy, 0.0) * jnp.exp(-vy * vy / temp), 0.0),
            axis=1,
            keepdims=True,
        )
        inward = sz.weight * along * across / (math.pi * temp)
        heat = jnp.where(entry == t, temp, heat)
        denom = jnp.where(entry == t, inward, denom)
    wall_ref[0:1, :] = alpha / (denom * (math.pi * heat))
    wall_ref[1:2, :] = 1.0 - alpha
    wall_ref[2:3, :] = heat
    wall_ref[3:SUB, :] = jnp.zeros((SUB - 3, sz.cells), jnp.float32)


def group_speed(sz, group):
    index = lax.broadcasted_iota(jnp.int32, (SUB, sz.cells), 0) + group * SUB
    return node_speed(index, sz.nx)


def first_kernel(sz, state, type_ref, index_ref, temps_ref, acc_ref, mirror, packet, right, left, wall):
    vert_index = lax.axis_index("vert")
    parity = vert_index % 2
    edges = Edges(sz, parity)
    wall_rows(sz, 1 - parity, type_ref, index_ref, temps_ref, acc_ref, wall)
    totals = zero_totals(sz)
    for positive in (False, True):
        out = right if positive else left

        def group_body(local, totals):
            group = local + (sz.half if positive else 0)
            rows = pl.ds(pl.multiple_of(group * SUB, SUB), SUB)
            sums = Moments((SUB, sz.cells))
            packers = [Packer(sz, edges, positive) for _ in range(2)]
            for k in range(sz.band):
                values = [state[f, k, rows, :] for f in range(2)]
                sums.add(*values)
                send_rows(sz, packers, values, k, local, group, mirror, out)
            return sums.finish(sz, vert_index, group_speed(sz, group), totals)

        totals = lax.fori_loop(0, sz.half, group_body, totals)
    put_moments(sz, vert_index, totals, packet, mirror)


def send_rows(sz, packers, values, k, local, group, mirror, side):
    for f in range(2):
        packers[f].add(values[f], k)
        if k % SUB == SUB - 1 or k == sz.band - 1:
            mirror[sz.mirror_index(f, group, k // SUB)] = packers[f].wall
        if k % sz.side_slots == sz.side_slots - 1 or k == sz.band - 1:
            side[f, local, k // sz.side_slots] = packers[f].side


def step_kernel(sz, last, *refs):
    refs = list(refs)
    state, mirror_in, right_in, left_in, packet_in, wall = refs[:6]
    others = refs[6 : 6 + sz.vert - 2]
    rest = refs[6 + sz.vert - 2 :]
    if last:
        (out, ey_ref, py_ref, cy_ref, c0_ref, y1_ref, y2_ref) = rest
    else:
        (out, mirror, packet, right, left, ey_ref, py_ref, cy_ref, c0_ref, y1_ref, y2_ref) = rest
    cells = sz.cells
    vert_index = lax.axis_index("vert")
    parity = vert_index % 2
    edges = Edges(sz, parity)
    even = parity == 0
    lane8 = lax.broadcasted_iota(jnp.int32, (SUB, cells), 1)

    blocks = sz.mirror_blocks
    tot = [packet_in[SUB * b : SUB * b + SUB, :] + mirror_in[blocks + b] for b in range(2)]
    for other in others:
        tot = [tot[b] + other[SUB * b : SUB * b + SUB, :] for b in range(2)]

    def row(r):
        return tot[r // SUB][r % SUB : r % SUB + 1, :]

    n, mx, my, energy, pxx, pxy, pyy, tx, ty = [row(r) for r in range(9)]
    inv_n = 1.0 / n
    ux, uy = mx * inv_n, my * inv_n
    usq = ux * ux + uy * uy
    theta = 2.0 / 3.0 * (energy * inv_n - usq)
    along = ux * mx + uy * my
    qx = tx - 2.0 * (ux * pxx + uy * pxy) + usq * mx - ux * energy + 2.0 * ux * along - ux * usq * n
    qy = ty - 2.0 * (ux * pxy + uy * pyy) + usq * my - uy * energy + 2.0 * uy * along - uy * usq * n
    inv_t = 1.0 / theta
    rate = (time_increment * relaxation_multiplier) * n * jnp.exp(shear_exponent * jnp.log(theta))
    amount = rate * n * inv_t * (1.0 / math.pi)
    flux_scale = (1.0 - diffusivity_ratio) * 0.8 * inv_n * inv_t * inv_t
    half_theta = jnp.broadcast_to(0.5 * theta, (SUB, cells))
    px, py = flux_scale * qx, flux_scale * qy

    vy = row_speed(sz, vert_index, lax.broadcasted_iota(jnp.int32, (sz.band, cells), 0))
    cy = vy - uy
    cy_sq = cy * cy * inv_t
    ey_ref[...] = amount * jnp.exp(-cy_sq)
    py_ref[...] = py * cy
    cy_ref[...] = cy_sq - 2.0
    b0, b1, b2 = beam_weights(vy)
    c0_ref[...] = (1.0 + b0) - rate
    y1_ref[...] = b1
    y2_ref[...] = b2

    y = lanes(sz) % Y
    flux = jnp.where(even, row(10), row(9))
    flux = jnp.where(y == jnp.where(even, Y - 1, 0), flux, 0.0)
    for span in (1, 2, 4, 8):
        flux = flux + roll(flux, jnp.where(even, cells - span, span))
    heat = wall[2:3, :]
    inv_heat = 1.0 / heat
    half_heat = jnp.broadcast_to(0.5 * heat, (SUB, cells))
    keep = jnp.broadcast_to(wall[1:2, :], (SUB, cells))
    emitted = flux * wall[0:1, :]
    wall_y = []
    for pack in range(sz.wall_packs):
        speed = row_speed(sz, vert_index, pack * SUB + y // 2)
        wall_y.append(jnp.broadcast_to(emitted * jnp.exp(-speed * speed * inv_heat), (SUB, cells)))

    totals = zero_totals(sz)
    for positive in (False, True):
        side_in = right_in if positive else left_in
        side_out = None if last else (right if positive else left)
        if positive:
            x_one, x_two = lane8 >= cells - Y, lane8 >= cells - 2 * Y
            x_shift = (Y, 2 * Y)
        else:
            x_one, x_two = lane8 < Y, lane8 < 2 * Y
            x_shift = (cells - Y, cells - 2 * Y)

        def group_body(local, totals):
            group = local + (sz.half if positive else 0)
            rows = pl.ds(pl.multiple_of(group * SUB, SUB), SUB)
            vx = group_speed(sz, group)
            cx = vx - ux
            cx_sq = cx * cx * inv_t
            ex = jnp.exp(-cx_sq)
            pxs = px * cx
            x0, x1, x2 = beam_weights(vx)
            wall_x = jnp.exp(-vx * vx * inv_heat)
            sums = Moments((SUB, cells))
            packers = [Packer(sz, edges, positive) for _ in range(2)]
            ghosts = sides = None
            for k in range(sz.band):
                slot = k % SUB
                if slot == 0:
                    diffuse = wall_x * wall_y[k // SUB]
                    ghosts = []
                    for f in range(2):
                        got = mirror_in[sz.mirror_index(f, group, k // SUB)]
                        got = jnp.where(edges.odd_lane == 1, roll(got, 1), roll(got, cells - 1))
                        ghosts.append(keep * got + (half_heat * diffuse if f else diffuse))
                side_slot = k % sz.side_slots
                if side_slot == 0:
                    sides = [side_in[f, local, k // sz.side_slots] for f in range(2)]
                shift = -2 * Y * side_slot
                if positive:
                    shift -= 2 * Y
                shift = shift % cells
                at = pl.ds(k, 1)
                maxwell = ex * ey_ref[at, :]
                p = pxs + py_ref[at, :]
                c2 = cx_sq + cy_ref[at, :]
                sg = maxwell * (1.0 + p * c2)
                sh = half_theta * (sg + p * maxwell)
                c0 = x0 + c0_ref[at, :]
                y1, y2 = y1_ref[at, :], y2_ref[at, :]
                values = []
                for f, source in ((0, sg), (1, sh)):
                    v = state[f, k, rows, :]
                    ghost = roll(ghosts[f], edges.unpack_shift(slot))
                    side = roll(sides[f], shift)
                    moved = v * c0 + source
                    moved = moved + x1 * roll(jnp.where(x_one, side, v), x_shift[0])
                    moved = moved + x2 * roll(jnp.where(x_two, side, v), x_shift[1])
                    moved = moved + y1 * roll(jnp.where(edges.one, ghost, v), edges.shift_one)
                    moved = moved + y2 * roll(jnp.where(edges.two, ghost, v), edges.shift_two)
                    out[f, k, rows, :] = moved
                    values.append(moved)
                if not last:
                    sums.add(*values)
                    send_rows(sz, packers, values, k, local, group, mirror, side_out)
            if last:
                return totals
            return sums.finish(sz, vert_index, vx, totals)

        totals = lax.fori_loop(0, sz.half, group_body, () if last else totals)
        totals = zero_totals(sz) if last else totals
    if not last:
        put_moments(sz, vert_index, totals, packet, mirror)


def shapes(sz):
    f32 = jnp.float32
    side = jax.ShapeDtypeStruct((2, sz.half, sz.side_packs, SUB, sz.cells), f32)
    return (
        jax.ShapeDtypeStruct((sz.mirror_blocks + 2, SUB, sz.cells), f32),
        jax.ShapeDtypeStruct((ROWS, sz.cells), f32),
        side,
        side,
    )


def on_device(distribution, wall_type, wall_temp_index, wall_temps, accommodation):
    _, band, nx, cells = distribution.shape
    vert = lax.axis_size("vert")
    columns = lax.axis_size("gx")
    sz = Sizes(band, nx, cells, vert)
    vmem = pl.BlockSpec(memory_space=pltpu.VMEM)
    smem = pl.BlockSpec(memory_space=pltpu.SMEM)
    state_shape = jax.ShapeDtypeStruct(distribution.shape, jnp.float32)
    bytes_moved = 2 * distribution.size * 4
    state = distribution
    mirror, packet, right, left, wall = pl.pallas_call(
        functools.partial(first_kernel, sz),
        out_shape=shapes(sz) + (jax.ShapeDtypeStruct((SUB, cells), jnp.float32),),
        in_specs=[vmem] + [smem] * 4,
        out_specs=(vmem,) * 5,
        cost_estimate=pl.CostEstimate(
            flops=10 * state.size, bytes_accessed=bytes_moved // 2, transcendentals=0
        ),
        name="first",
    )(state, wall_type, wall_temp_index, wall_temps, accommodation)
    ring = [(i, (i + 1) % columns) for i in range(columns)]
    back = [(j, i) for i, j in ring]
    for iteration in range(ITERS):
        last = iteration == ITERS - 1
        mirror_in = lax.ppermute(mirror, "vert", [(s, s ^ 1) for s in range(vert)])
        right_in = lax.ppermute(right, "gx", ring)
        left_in = lax.ppermute(left, "gx", back)
        others = []
        for mask in range(vert - 1, 1, -1):
            others.append(lax.ppermute(packet, "vert", [(s, s ^ mask) for s in range(vert)]))
        result = pl.pallas_call(
            functools.partial(step_kernel, sz, last),
            out_shape=(state_shape,) if last else (state_shape,) + shapes(sz),
            in_specs=[vmem] * (6 + len(others)),
            out_specs=(vmem,) if last else (vmem,) * 5,
            scratch_shapes=[pltpu.VMEM((band, cells), jnp.float32)] * 6,
            cost_estimate=pl.CostEstimate(
                flops=40 * state.size, bytes_accessed=bytes_moved, transcendentals=0
            ),
            name="last" if last else "step",
        )(state, mirror_in, right_in, left_in, packet, wall, *others)
        if last:
            (state,) = result
        else:
            state, mirror, packet, right, left = result
    return state


def solution(mesh):
    placed = (P(None, "vert", None, "gx"), P(None, "gx"), P(None, "gx"), P(), P())
    return jax.shard_map(
        on_device,
        mesh=mesh,
        in_specs=placed,
        out_specs=P(None, "vert", None, "gx"),
        check_vma=False,
    )
```

```python
import functools
import math

import jax
import jax.numpy as jnp
from jax import lax
from jax.experimental import pallas as pl
from jax.experimental.pallas import tpu as pltpu
from jax.sharding import PartitionSpec as P


Y = 16
ITERS = 4
NTEMP = 2
NTYPE = 3
SUB = 8
LANES = 128
ROWS = 16
PART_X = 16
PART_K = LANES // PART_X
FIELDS = 9
KERNEL_VMEM = 16 * 1024 * 1024
highest = lax.Precision.HIGHEST

vmax_speed = 4.5
courant = 0.5
diffusivity_ratio = 2.0 / 3.0
relaxation_multiplier = 2.5
shear_exponent = 0.19
time_increment = courant / vmax_speed


class Sizes:
    def __init__(self, band, nx, cells, vert):
        assert cells == SUB * Y and nx % (2 * PART_X) == 0
        self.band, self.nx, self.cells, self.vert = band, nx, cells, vert
        self.nv = band * vert
        self.xg = nx // PART_X
        self.kg = -(-band // PART_K)
        self.tiles = self.xg * self.kg
        self.half = self.tiles // 2
        self.state_rows = 2 * self.tiles * cells
        self.side_rows = 2 * self.half * Y * 2 + 2 * SUB
        self.mirror_blocks = 4 * self.tiles
        self.weight = 2.0 * vmax_speed / nx * (2.0 * vmax_speed / self.nv)

    def base(self, f, t):
        return (f * self.tiles + t) * self.cells

    def side_base(self, f, t):
        return SUB + (f * self.half + t % self.half) * 2 * Y

    def mirror_index(self, d, f, t):
        return (d * 2 + f) * self.tiles + t


def node_speed(index, number):
    return vmax_speed * (2.0 * index.astype(jnp.float32) + 1.0 - number) / number


def row_speed(sz, vert_index, offset):
    lower = vert_index // 2 * sz.band + offset
    return node_speed(jnp.where(vert_index % 2 == 0, lower, sz.nv - 1 - lower), sz.nv)


def beam_weights(speed):
    s = jnp.abs(speed) * time_increment
    return -1.5 * s + 0.5 * s * s, 2.0 * s - s * s, -0.5 * s + 0.5 * s * s


def lane():
    return lax.broadcasted_iota(jnp.int32, (SUB, LANES), 1)


def sub():
    return lax.broadcasted_iota(jnp.int32, (SUB, LANES), 0)


def x_speed(sz, group):
    return node_speed(group * PART_X + lane() % PART_X, sz.nx)


def y_speed(sz, vert_index, group):
    return row_speed(sz, vert_index, group * PART_K + lane() // PART_X)


def inside(sz, group):
    if (group + 1) * PART_K <= sz.band:
        return None
    return group * PART_K + lane() // PART_X < sz.band


def masked(mask, value):
    return value if mask is None else jnp.where(mask, value, 0.0)


def real_row(parity, step):
    return jnp.where(parity == 0, Y - 1 - step, step)


def block(start):
    return pl.ds(pl.multiple_of(start, SUB), SUB)


def add_columns(vy, g, h, sums):
    p = vy * g
    q = vy * p
    r = vy * (q + h)
    new = (g, p, q, r, h)
    return new if sums is None else tuple(a + b for a, b in zip(sums, new))


def add_group(vx, sums, totals):
    t0, t1, t2, t3, u0 = sums
    a = vx * t0
    b = vx * a
    c = vx * t1
    new = (t0, a, t1, b, c, t2, u0, vx * (b + t2 + u0), vx * c + t3)
    return new if totals is None else tuple(x + y for x, y in zip(totals, new))


def put_sums(sums_ref, y, totals):
    for m, total in enumerate(totals):
        sums_ref[m, block(y * SUB), :] = total


def send(sz, vert_index, state, sums_ref, mirror, packet, right, left):
    rows = []
    for m in range(FIELDS):
        rows.append(jnp.sum(sums_ref[m].T, axis=0, keepdims=True) * sz.weight)
    n, mx, my, pxx, pxy, pyy, extra, tx, ty = rows
    even = vert_index % 2 == 0
    zero = jnp.zeros_like(n)
    rows = [n, mx, my, pxx + pyy + extra, pxx, pxy, pyy, tx, ty]
    rows += [jnp.where(even, -my, zero), jnp.where(even, zero, my)]
    rows += [zero] * (ROWS - len(rows))
    for r, value in enumerate(rows):
        packet[r : r + 1, :] = value
        mirror[sz.mirror_blocks + r // SUB, r % SUB : r % SUB + 1, :] = value
    for f in range(2):
        for t in range(sz.tiles):
            base = sz.base(f, t)
            for d in range(2):
                mirror[sz.mirror_index(d, f, t)] = state[pl.ds(base + (Y - 1 - d) * SUB, SUB), :]
            positive = t >= sz.half
            out, first = (right, SUB - 2) if positive else (left, 0)
            side = sz.side_base(f, t)
            for c in range(2):
                for part in range(0, Y, SUB):
                    edge = state[pl.ds(base + part * SUB + first + c, SUB, stride=SUB), :]
                    out[pl.ds(side + 2 * part + c, SUB, stride=2), :] = edge
    pad = jnp.zeros((SUB, LANES), jnp.float32)
    for out in (right, left):
        out[0:SUB, :] = pad
        out[sz.side_rows - SUB : sz.side_rows, :] = pad


def wall_fields(sz, face, type_ref, index_ref, temps_ref, acc_ref, wall):
    column = sub()
    kind = jnp.zeros_like(column)
    entry = jnp.zeros_like(column)
    for x in range(SUB):
        kind = jnp.where(column == x, type_ref[face, x], kind)
        entry = jnp.where(column == x, index_ref[face, x], entry)
    percent = jnp.zeros_like(column)
    for t in range(NTYPE):
        percent = jnp.where(kind == t, acc_ref[t], percent)
    alpha = percent.astype(jnp.float32) / 100.0
    heat = jnp.ones((SUB, LANES), jnp.float32)
    denom = jnp.ones((SUB, LANES), jnp.float32)

    def grid(number):
        index = lax.broadcasted_iota(jnp.int32, (1, -(-number // LANES) * LANES), 1)
        return node_speed(index, number), index < number

    vx, in_x = grid(sz.nx)
    vy, in_y = grid(sz.nv)
    for t in range(NTEMP):
        temp = jnp.full((1, 1), temps_ref[t], jnp.float32)
        along = jnp.sum(jnp.where(in_x, jnp.exp(-vx * vx / temp), 0.0), axis=1, keepdims=True)
        across = jnp.sum(
            jnp.where(in_y, jnp.maximum(vy, 0.0) * jnp.exp(-vy * vy / temp), 0.0),
            axis=1,
            keepdims=True,
        )
        inward = sz.weight * along * across / (math.pi * temp)
        heat = jnp.where(entry == t, temp, heat)
        denom = jnp.where(entry == t, inward, denom)
    wall[0] = alpha / (denom * (math.pi * heat))
    wall[1] = 1.0 - alpha
    wall[2] = heat


def first_kernel(
    sz, given, type_ref, index_ref, temps_ref, acc_ref,
    state, mirror, packet, right, left, wall, sums_ref, turn,
):
    vert_index = lax.axis_index("vert")
    parity = vert_index % 2
    wall_fields(sz, 1 - parity, type_ref, index_ref, temps_ref, acc_ref, wall)
    for f in range(2):
        for xg in range(sz.xg):
            for kg in range(sz.kg):
                parts = []
                for k in range(kg * PART_K, (kg + 1) * PART_K):
                    if k < sz.band:
                        parts.append(given[f, k, xg * PART_X : (xg + 1) * PART_X, :])
                    else:
                        parts.append(jnp.zeros((PART_X, sz.cells), jnp.float32))
                turned = jnp.concatenate(parts, axis=0).T
                t = xg * sz.kg + kg
                slot = t % 2
                for x in range(SUB):
                    for part in range(0, Y, SUB):
                        piece = turned[x * Y + part : x * Y + part + SUB, :]
                        turn[slot, pl.ds(part * SUB + x, SUB, stride=SUB), :] = piece
                base = sz.base(f, t)
                for step in range(Y):
                    y = real_row(parity, step)
                    state[pl.ds(base + step * SUB, SUB), :] = turn[slot, block(y * SUB), :]

    def step_body(step, carry):
        totals = None
        for xg in range(sz.xg):
            sums = None
            for kg in range(sz.kg):
                g, h = [state[block(sz.base(f, xg * sz.kg + kg) + step * SUB), :] for f in range(2)]
                sums = add_columns(y_speed(sz, vert_index, kg), g, h, sums)
            totals = add_group(x_speed(sz, xg), sums, totals)
        put_sums(sums_ref, real_row(parity, step), totals)
        return carry

    lax.fori_loop(0, Y, step_body, 0)
    send(sz, vert_index, state, sums_ref, mirror, packet, right, left)


def fields_of(parity, tot):
    def row(r):
        return tot[r // SUB][r % SUB : r % SUB + 1, :]

    n, mx, my, energy, pxx, pxy, pyy, tx, ty = [row(r) for r in range(9)]
    inv_n = 1.0 / n
    ux, uy = mx * inv_n, my * inv_n
    usq = ux * ux + uy * uy
    theta = 2.0 / 3.0 * (energy * inv_n - usq)
    along = ux * mx + uy * my
    qx = tx - 2.0 * (ux * pxx + uy * pxy) + usq * mx - ux * energy + 2.0 * ux * along - ux * usq * n
    qy = ty - 2.0 * (ux * pxy + uy * pyy) + usq * my - uy * energy + 2.0 * uy * along - uy * usq * n
    inv_t = 1.0 / theta
    rate = (time_increment * relaxation_multiplier) * n * jnp.exp(shear_exponent * jnp.log(theta))
    amount = rate * n * inv_t * (1.0 / math.pi)
    scale = (1.0 - diffusivity_ratio) * 0.8 * inv_n * inv_t * inv_t
    flux = jnp.where(parity == 0, row(10), row(9))
    return [ux, uy, inv_t, amount, scale * qx, scale * qy, 0.5 * theta, rate, flux]


def step_kernel(sz, last, *refs):
    refs = list(refs)
    state, mirror_in, right_in, left_in, packet_in, wall = refs[:6]
    others = refs[6 : 6 + sz.vert - 2]
    rest = refs[6 + sz.vert - 2 :]
    if last:
        (final, spread, ghosts, xw, yw, out, turn) = rest
    else:
        (out, mirror, packet, right, left, spread, ghosts, xw, yw, sums_ref) = rest
    vert_index = lax.axis_index("vert")
    parity = vert_index % 2

    tot = [packet_in[SUB * b : SUB * b + SUB, :] + mirror_in[sz.mirror_blocks + b] for b in range(2)]
    for other in others:
        tot = [tot[b] + other[SUB * b : SUB * b + SUB, :] for b in range(2)]
    rows = fields_of(parity, tot)
    index = lax.broadcasted_iota(jnp.int32, (ROWS, LANES), 0)
    table = jnp.zeros((ROWS, sz.cells), jnp.float32)
    for r, value in enumerate(rows):
        table = jnp.where(index == r, value, table)
    for r in range(FIELDS):
        pick = (index == r).astype(jnp.float32)
        spread[r] = lax.dot_general(
            table, pick, (((0,), (0,)), ((), ())),
            precision=highest, preferred_element_type=jnp.float32,
        )

    for xg in range(sz.xg):
        speed = x_speed(sz, xg)
        for r, value in enumerate((speed,) + beam_weights(speed)):
            xw[4 * xg + r] = value
    for kg in range(sz.kg):
        speed = y_speed(sz, vert_index, kg)
        for r, value in enumerate((speed,) + beam_weights(speed)):
            yw[4 * kg + r] = value

    inv_heat = 1.0 / wall[2]
    half_heat = 0.5 * wall[2]
    keep = wall[1]
    emitted = spread[FIELDS - 1, block(real_row(parity, 0) * SUB), :] * wall[0]
    wall_y = []
    for kg in range(sz.kg):
        vy = yw[4 * kg]
        wall_y.append(masked(inside(sz, kg), emitted * jnp.exp(-vy * vy * inv_heat)))
    for xg in range(sz.xg):
        vx = xw[4 * xg]
        wall_x = jnp.exp(-vx * vx * inv_heat)
        for kg in range(sz.kg):
            diffuse = wall_x * wall_y[kg]
            t = xg * sz.kg + kg
            for f in range(2):
                add = half_heat * diffuse if f else diffuse
                for d in range(2):
                    at = sz.mirror_index(d, f, t)
                    ghosts[at] = keep * mirror_in[at] + add

    column = sub()

    def advance(step, upstream):
        y = real_row(parity, step)
        ux, uy, inv_t, amount, px, py, half_theta, rate = [
            spread[r, block(y * SUB), :] for r in range(FIELDS - 1)
        ]
        along_y = []
        for kg in range(sz.kg):
            cy = yw[4 * kg] - uy
            cy_sq = cy * cy * inv_t
            along_y.append((masked(inside(sz, kg), amount * jnp.exp(-cy_sq)), py * cy, cy_sq - 2.0))
        totals = None
        for xg in range(sz.xg):
            vx = xw[4 * xg]
            cx = vx - ux
            cx_sq = cx * cx * inv_t
            ex = jnp.exp(-cx_sq)
            pxs = px * cx
            x0 = (1.0 + xw[4 * xg + 1]) - rate
            x1, x2 = xw[4 * xg + 2], xw[4 * xg + 3]
            sums = None
            for kg in range(sz.kg):
                t = xg * sz.kg + kg
                positive = t >= sz.half
                ey, pys, cys = along_y[kg]
                maxwell = ex * ey
                p = pxs + pys
                sg = maxwell * (1.0 + p * (cx_sq + cys))
                sh = half_theta * (sg + p * maxwell)
                c0 = x0 + yw[4 * kg + 1]
                y1, y2 = yw[4 * kg + 2], yw[4 * kg + 3]
                values = []
                for f, source in ((0, sg), (1, sh)):
                    at = sz.base(f, t) + step * SUB
                    side = sz.side_base(f, t) + 2 * step
                    v = state[block(at), :]
                    if positive:
                        one = jnp.where(column < 1, right_in[pl.ds(side + 1, SUB), :], state[pl.ds(at - 1, SUB), :])
                        two = jnp.where(column < 2, right_in[pl.ds(side, SUB), :], state[pl.ds(at - 2, SUB), :])
                    else:
                        one = jnp.where(
                            column >= SUB - 1, left_in[pl.ds(side - (SUB - 1), SUB), :], state[pl.ds(at + 1, SUB), :]
                        )
                        two = jnp.where(
                            column >= SUB - 2, left_in[pl.ds(side - (SUB - 2), SUB), :], state[pl.ds(at + 2, SUB), :]
                        )
                    near, far = upstream(f, t, at)
                    moved = (v * c0 + source) + (x1 * one + x2 * two) + (y1 * near + y2 * far)
                    out[block(at), :] = moved
                    values.append(moved)
                if not last:
                    sums = add_columns(yw[4 * kg], values[0], values[1], sums)
            if not last:
                totals = add_group(vx, sums, totals)
        if not last:
            put_sums(sums_ref, y, totals)

    def ghost(d, f, t):
        return ghosts[sz.mirror_index(d, f, t)]

    advance(0, lambda f, t, at: (ghost(0, f, t), ghost(1, f, t)))
    advance(1, lambda f, t, at: (state[block(at - SUB), :], ghost(0, f, t)))

    def body(step, carry):
        advance(step, lambda f, t, at: (state[block(at - SUB), :], state[block(at - 2 * SUB), :]))
        return carry

    lax.fori_loop(2, Y, body, 0)
    if not last:
        send(sz, vert_index, out, sums_ref, mirror, packet, right, left)
        return
    for f in range(2):
        for xg in range(sz.xg):
            for kg in range(sz.kg):
                t = xg * sz.kg + kg
                slot = t % 2
                base = sz.base(f, t)
                for step in range(Y):
                    y = real_row(parity, step)
                    turn[slot, block(y * SUB), :] = out[pl.ds(base + step * SUB, SUB), :]
                parts = []
                for x in range(SUB):
                    for part in range(0, Y, SUB):
                        parts.append(turn[slot, pl.ds(part * SUB + x, SUB, stride=SUB), :])
                turned = jnp.concatenate(parts, axis=0).T
                for k in range(kg * PART_K, min((kg + 1) * PART_K, sz.band)):
                    row = (k - kg * PART_K) * PART_X
                    final[f, k, xg * PART_X : (xg + 1) * PART_X, :] = turned[row : row + PART_X, :]


def shapes(sz):
    f32 = jnp.float32
    side = jax.ShapeDtypeStruct((sz.side_rows, LANES), f32)
    return (
        jax.ShapeDtypeStruct((sz.state_rows, LANES), f32),
        jax.ShapeDtypeStruct((sz.mirror_blocks + 2, SUB, LANES), f32),
        jax.ShapeDtypeStruct((ROWS, sz.cells), f32),
        side,
        side,
    )


def on_device(distribution, wall_type, wall_temp_index, wall_temps, accommodation):
    _, band, nx, cells = distribution.shape
    vert = lax.axis_size("vert")
    columns = lax.axis_size("gx")
    sz = Sizes(band, nx, cells, vert)
    vmem = pl.BlockSpec(memory_space=pltpu.VMEM)
    smem = pl.BlockSpec(memory_space=pltpu.SMEM)
    final_shape = jax.ShapeDtypeStruct(distribution.shape, jnp.float32)
    bytes_moved = 2 * distribution.size * 4
    sums_scratch = pltpu.VMEM((FIELDS, sz.cells, LANES), jnp.float32)
    turn_scratch = pltpu.VMEM((2, sz.cells, LANES), jnp.float32)
    step_scratch = [
        pltpu.VMEM((FIELDS, sz.cells, LANES), jnp.float32),
        pltpu.VMEM((sz.mirror_blocks, SUB, LANES), jnp.float32),
        pltpu.VMEM((4 * sz.xg, SUB, LANES), jnp.float32),
        pltpu.VMEM((4 * sz.kg, SUB, LANES), jnp.float32),
    ]
    state, mirror, packet, right, left, wall = pl.pallas_call(
        functools.partial(first_kernel, sz),
        out_shape=shapes(sz) + (jax.ShapeDtypeStruct((3, SUB, LANES), jnp.float32),),
        in_specs=[vmem] + [smem] * 4,
        out_specs=(vmem,) * 6,
        scratch_shapes=[sums_scratch, turn_scratch],
        cost_estimate=pl.CostEstimate(
            flops=10 * distribution.size, bytes_accessed=bytes_moved, transcendentals=0
        ),
        compiler_params=pltpu.CompilerParams(vmem_limit_bytes=KERNEL_VMEM),
        name="first",
    )(distribution, wall_type, wall_temp_index, wall_temps, accommodation)
    ring = [(i, (i + 1) % columns) for i in range(columns)]
    back = [(j, i) for i, j in ring]
    for iteration in range(ITERS):
        last = iteration == ITERS - 1
        mirror_in = lax.ppermute(mirror, "vert", [(s, s ^ 1) for s in range(vert)])
        right_in = lax.ppermute(right, "gx", ring)
        left_in = lax.ppermute(left, "gx", back)
        others = []
        for mask in range(vert - 1, 1, -1):
            others.append(lax.ppermute(packet, "vert", [(s, s ^ mask) for s in range(vert)]))
        if last:
            scratch = step_scratch + [pltpu.VMEM((sz.state_rows, LANES), jnp.float32), turn_scratch]
        else:
            scratch = step_scratch + [sums_scratch]
        result = pl.pallas_call(
            functools.partial(step_kernel, sz, last),
            out_shape=(final_shape,) if last else shapes(sz),
            in_specs=[vmem] * (6 + len(others)),
            out_specs=(vmem,) if last else (vmem,) * 5,
            scratch_shapes=scratch,
            cost_estimate=pl.CostEstimate(
                flops=40 * distribution.size, bytes_accessed=bytes_moved, transcendentals=0
            ),
            compiler_params=pltpu.CompilerParams(vmem_limit_bytes=KERNEL_VMEM),
            name="last" if last else "step",
        )(state, mirror_in, right_in, left_in, packet, wall, *others)
        if last:
            (state,) = result
        else:
            state, mirror, packet, right, left = result
    return state


def solution(mesh):
    placed = (P(None, "vert", None, "gx"), P(None, "gx"), P(None, "gx"), P(), P())
    return jax.shard_map(
        on_device,
        mesh=mesh,
        in_specs=placed,
        out_specs=P(None, "vert", None, "gx"),
        check_vma=False,
    )
```

```python
import functools
import math

import jax
import jax.numpy as jnp
from jax import lax
from jax.experimental import pallas as pl
from jax.experimental.pallas import tpu as pltpu
from jax.sharding import PartitionSpec as P


Y = 16
ITERS = 4
NTEMP = 2
NTYPE = 3
SUB = 8
LANES = 128
ROWS = 16
PART_X = 16
PART_K = LANES // PART_X
FIELDS = 9
KERNEL_VMEM = 16 * 1024 * 1024
ALL_VMEM = 64 * 1024 * 1024
highest = lax.Precision.HIGHEST

vmax_speed = 4.5
courant = 0.5
diffusivity_ratio = 2.0 / 3.0
relaxation_multiplier = 2.5
shear_exponent = 0.19
time_increment = courant / vmax_speed


class Sizes:
    def __init__(self, band, nx, cells, vert):
        assert cells == SUB * Y and nx % (2 * PART_X) == 0
        self.band, self.nx, self.cells, self.vert = band, nx, cells, vert
        self.nv = band * vert
        self.xg = nx // PART_X
        self.kg = -(-band // PART_K)
        self.tiles = self.xg * self.kg
        self.half = self.tiles // 2
        self.state_rows = 2 * self.tiles * cells
        self.side_rows = 2 * self.half * Y * 2 + 2 * SUB
        self.mirror_blocks = 4 * self.tiles
        self.weight = 2.0 * vmax_speed / nx * (2.0 * vmax_speed / self.nv)

    def base(self, f, t):
        return (f * self.tiles + t) * self.cells

    def side_base(self, f, t):
        return SUB + (f * self.half + t % self.half) * 2 * Y

    def mirror_index(self, d, f, t):
        return (d * 2 + f) * self.tiles + t


def node_speed(index, number):
    return vmax_speed * (2.0 * index.astype(jnp.float32) + 1.0 - number) / number


def row_speed(sz, vert_index, offset):
    lower = vert_index // 2 * sz.band + offset
    return node_speed(jnp.where(vert_index % 2 == 0, lower, sz.nv - 1 - lower), sz.nv)


def beam_weights(speed):
    s = jnp.abs(speed) * time_increment
    return -1.5 * s + 0.5 * s * s, 2.0 * s - s * s, -0.5 * s + 0.5 * s * s


def lane():
    return lax.broadcasted_iota(jnp.int32, (SUB, LANES), 1)


def sub():
    return lax.broadcasted_iota(jnp.int32, (SUB, LANES), 0)


def x_speed(sz, group):
    return node_speed(group * PART_X + lane() % PART_X, sz.nx)


def y_speed(sz, vert_index, group):
    return row_speed(sz, vert_index, group * PART_K + lane() // PART_X)


def inside(sz, group):
    if (group + 1) * PART_K <= sz.band:
        return None
    return group * PART_K + lane() // PART_X < sz.band


def masked(mask, value):
    return value if mask is None else jnp.where(mask, value, 0.0)


def real_row(parity, step):
    return jnp.where(parity == 0, Y - 1 - step, step)


def block(start):
    return pl.ds(pl.multiple_of(start, SUB), SUB)


def add_columns(vy, g, h, sums):
    p = vy * g
    q = vy * p
    r = vy * (q + h)
    new = (g, p, q, r, h)
    return new if sums is None else tuple(a + b for a, b in zip(sums, new))


def add_group(vx, sums, totals):
    t0, t1, t2, t3, u0 = sums
    a = vx * t0
    b = vx * a
    c = vx * t1
    new = (t0, a, t1, b, c, t2, u0, vx * (b + t2 + u0), vx * c + t3)
    return new if totals is None else tuple(x + y for x, y in zip(totals, new))


def put_sums(sums_ref, y, totals):
    for m, total in enumerate(totals):
        sums_ref[m, block(y * SUB), :] = total


def send(sz, vert_index, state, sums_ref, mirror, packet, right, left):
    rows = []
    for m in range(FIELDS):
        rows.append(jnp.sum(sums_ref[m].T, axis=0, keepdims=True) * sz.weight)
    n, mx, my, pxx, pxy, pyy, extra, tx, ty = rows
    even = vert_index % 2 == 0
    zero = jnp.zeros_like(n)
    rows = [n, mx, my, pxx + pyy + extra, pxx, pxy, pyy, tx, ty]
    rows += [jnp.where(even, -my, zero), jnp.where(even, zero, my)]
    rows += [zero] * (ROWS - len(rows))
    for r, value in enumerate(rows):
        packet[r : r + 1, :] = value
        mirror[sz.mirror_blocks + r // SUB, r % SUB : r % SUB + 1, :] = value
    for f in range(2):
        for t in range(sz.tiles):
            base = sz.base(f, t)
            for d in range(2):
                mirror[sz.mirror_index(d, f, t)] = state[pl.ds(base + (Y - 1 - d) * SUB, SUB), :]
            positive = t >= sz.half
            out, first = (right, SUB - 2) if positive else (left, 0)
            side = sz.side_base(f, t)
            for c in range(2):
                for part in range(0, Y, SUB):
                    edge = state[pl.ds(base + part * SUB + first + c, SUB, stride=SUB), :]
                    out[pl.ds(side + 2 * part + c, SUB, stride=2), :] = edge
    pad = jnp.zeros((SUB, LANES), jnp.float32)
    for out in (right, left):
        out[0:SUB, :] = pad
        out[sz.side_rows - SUB : sz.side_rows, :] = pad


def wall_kernel(sz, type_ref, index_ref, temps_ref, acc_ref, wall):
    face = 1 - lax.axis_index("vert") % 2
    column = sub()
    kind = jnp.zeros_like(column)
    entry = jnp.zeros_like(column)
    for x in range(SUB):
        kind = jnp.where(column == x, type_ref[face, x], kind)
        entry = jnp.where(column == x, index_ref[face, x], entry)
    percent = jnp.zeros_like(column)
    for t in range(NTYPE):
        percent = jnp.where(kind == t, acc_ref[t], percent)
    alpha = percent.astype(jnp.float32) / 100.0
    heat = jnp.ones((SUB, LANES), jnp.float32)
    denom = jnp.ones((SUB, LANES), jnp.float32)

    def grid(number):
        index = lax.broadcasted_iota(jnp.int32, (1, -(-number // LANES) * LANES), 1)
        return node_speed(index, number), index < number

    vx, in_x = grid(sz.nx)
    vy, in_y = grid(sz.nv)
    for t in range(NTEMP):
        temp = jnp.full((1, 1), temps_ref[t], jnp.float32)
        along = jnp.sum(jnp.where(in_x, jnp.exp(-vx * vx / temp), 0.0), axis=1, keepdims=True)
        across = jnp.sum(
            jnp.where(in_y, jnp.maximum(vy, 0.0) * jnp.exp(-vy * vy / temp), 0.0),
            axis=1,
            keepdims=True,
        )
        inward = sz.weight * along * across / (math.pi * temp)
        heat = jnp.where(entry == t, temp, heat)
        denom = jnp.where(entry == t, inward, denom)
    wall[0] = alpha / (denom * (math.pi * heat))
    wall[1] = 1.0 - alpha
    wall[2] = heat


def chunk_copy(sz, source, target, sems, f, kg):
    rows = pl.ds(kg * PART_K, min(PART_K, sz.band - kg * PART_K))
    return pltpu.make_async_copy(
        source.at[f, rows], target.at[f, rows], sems.at[f * sz.kg + kg]
    )


def first_kernel(sz, argument, state, mirror, packet, right, left, sums_ref, turn, given, sems):
    vert_index = lax.axis_index("vert")
    parity = vert_index % 2
    for f in range(2):
        for kg in range(sz.kg):
            chunk_copy(sz, argument, given, sems, f, kg).start()
    for f in range(2):
        for kg in range(sz.kg):
            chunk_copy(sz, argument, given, sems, f, kg).wait()
            for xg in range(sz.xg):
                parts = []
                for k in range(kg * PART_K, (kg + 1) * PART_K):
                    if k < sz.band:
                        parts.append(given[f, k, xg * PART_X : (xg + 1) * PART_X, :])
                    else:
                        parts.append(jnp.zeros((PART_X, sz.cells), jnp.float32))
                turned = jnp.concatenate(parts, axis=0).T
                t = xg * sz.kg + kg
                slot = xg % 2
                for x in range(SUB):
                    for part in range(0, Y, SUB):
                        piece = turned[x * Y + part : x * Y + part + SUB, :]
                        turn[slot, pl.ds(part * SUB + x, SUB, stride=SUB), :] = piece
                base = sz.base(f, t)
                for step in range(Y):
                    y = real_row(parity, step)
                    state[pl.ds(base + step * SUB, SUB), :] = turn[slot, block(y * SUB), :]

    def step_body(step, carry):
        totals = None
        for xg in range(sz.xg):
            sums = None
            for kg in range(sz.kg):
                g, h = [state[block(sz.base(f, xg * sz.kg + kg) + step * SUB), :] for f in range(2)]
                sums = add_columns(y_speed(sz, vert_index, kg), g, h, sums)
            totals = add_group(x_speed(sz, xg), sums, totals)
        put_sums(sums_ref, real_row(parity, step), totals)
        return carry

    lax.fori_loop(0, Y, step_body, 0)
    send(sz, vert_index, state, sums_ref, mirror, packet, right, left)


def fields_of(parity, tot):
    def row(r):
        return tot[r // SUB][r % SUB : r % SUB + 1, :]

    n, mx, my, energy, pxx, pxy, pyy, tx, ty = [row(r) for r in range(9)]
    inv_n = 1.0 / n
    ux, uy = mx * inv_n, my * inv_n
    usq = ux * ux + uy * uy
    theta = 2.0 / 3.0 * (energy * inv_n - usq)
    along = ux * mx + uy * my
    qx = tx - 2.0 * (ux * pxx + uy * pxy) + usq * mx - ux * energy + 2.0 * ux * along - ux * usq * n
    qy = ty - 2.0 * (ux * pxy + uy * pyy) + usq * my - uy * energy + 2.0 * uy * along - uy * usq * n
    inv_t = 1.0 / theta
    rate = (time_increment * relaxation_multiplier) * n * jnp.exp(shear_exponent * jnp.log(theta))
    amount = rate * n * inv_t * (1.0 / math.pi)
    scale = (1.0 - diffusivity_ratio) * 0.8 * inv_n * inv_t * inv_t
    flux = jnp.where(parity == 0, row(10), row(9))
    return [ux, uy, inv_t, amount, scale * qx, scale * qy, 0.5 * theta, rate, flux]


def step_kernel(sz, last, *refs):
    refs = list(refs)
    state, mirror_in, right_in, left_in, packet_in, wall = refs[:6]
    others = refs[6 : 6 + sz.vert - 2]
    rest = refs[6 + sz.vert - 2 :]
    if last:
        (result, spread, ghosts, xw, yw, out, turn, final, sems) = rest
    else:
        (out, mirror, packet, right, left, spread, ghosts, xw, yw, sums_ref) = rest
    vert_index = lax.axis_index("vert")
    parity = vert_index % 2

    tot = [packet_in[SUB * b : SUB * b + SUB, :] + mirror_in[sz.mirror_blocks + b] for b in range(2)]
    for other in others:
        tot = [tot[b] + other[SUB * b : SUB * b + SUB, :] for b in range(2)]
    rows = fields_of(parity, tot)
    index = lax.broadcasted_iota(jnp.int32, (ROWS, LANES), 0)
    table = jnp.zeros((ROWS, sz.cells), jnp.float32)
    for r, value in enumerate(rows):
        table = jnp.where(index == r, value, table)
    for r in range(FIELDS):
        pick = (index == r).astype(jnp.float32)
        spread[r] = lax.dot_general(
            table, pick, (((0,), (0,)), ((), ())),
            precision=highest, preferred_element_type=jnp.float32,
        )

    for xg in range(sz.xg):
        speed = x_speed(sz, xg)
        for r, value in enumerate((speed,) + beam_weights(speed)):
            xw[4 * xg + r] = value
    for kg in range(sz.kg):
        speed = y_speed(sz, vert_index, kg)
        for r, value in enumerate((speed,) + beam_weights(speed)):
            yw[4 * kg + r] = value

    inv_heat = 1.0 / wall[2]
    half_heat = 0.5 * wall[2]
    keep = wall[1]
    emitted = spread[FIELDS - 1, block(real_row(parity, 0) * SUB), :] * wall[0]
    wall_y = []
    for kg in range(sz.kg):
        vy = yw[4 * kg]
        wall_y.append(masked(inside(sz, kg), emitted * jnp.exp(-vy * vy * inv_heat)))
    for xg in range(sz.xg):
        vx = xw[4 * xg]
        wall_x = jnp.exp(-vx * vx * inv_heat)
        for kg in range(sz.kg):
            diffuse = wall_x * wall_y[kg]
            t = xg * sz.kg + kg
            for f in range(2):
                add = half_heat * diffuse if f else diffuse
                for d in range(2):
                    at = sz.mirror_index(d, f, t)
                    ghosts[at] = keep * mirror_in[at] + add

    column = sub()

    def advance(step, upstream):
        y = real_row(parity, step)
        ux, uy, inv_t, amount, px, py, half_theta, rate = [
            spread[r, block(y * SUB), :] for r in range(FIELDS - 1)
        ]
        along_y = []
        for kg in range(sz.kg):
            cy = yw[4 * kg] - uy
            cy_sq = cy * cy * inv_t
            along_y.append((masked(inside(sz, kg), amount * jnp.exp(-cy_sq)), py * cy, cy_sq - 2.0))
        totals = None
        for xg in range(sz.xg):
            vx = xw[4 * xg]
            cx = vx - ux
            cx_sq = cx * cx * inv_t
            ex = jnp.exp(-cx_sq)
            pxs = px * cx
            x0 = (1.0 + xw[4 * xg + 1]) - rate
            x1, x2 = xw[4 * xg + 2], xw[4 * xg + 3]
            sums = None
            for kg in range(sz.kg):
                t = xg * sz.kg + kg
                positive = t >= sz.half
                ey, pys, cys = along_y[kg]
                maxwell = ex * ey
                p = pxs + pys
                sg = maxwell * (1.0 + p * (cx_sq + cys))
                sh = half_theta * (sg + p * maxwell)
                c0 = x0 + yw[4 * kg + 1]
                y1, y2 = yw[4 * kg + 2], yw[4 * kg + 3]
                values = []
                for f, source in ((0, sg), (1, sh)):
                    at = sz.base(f, t) + step * SUB
                    side = sz.side_base(f, t) + 2 * step
                    v = state[block(at), :]
                    if positive:
                        one = jnp.where(column < 1, right_in[pl.ds(side + 1, SUB), :], state[pl.ds(at - 1, SUB), :])
                        two = jnp.where(column < 2, right_in[pl.ds(side, SUB), :], state[pl.ds(at - 2, SUB), :])
                    else:
                        one = jnp.where(
                            column >= SUB - 1, left_in[pl.ds(side - (SUB - 1), SUB), :], state[pl.ds(at + 1, SUB), :]
                        )
                        two = jnp.where(
                            column >= SUB - 2, left_in[pl.ds(side - (SUB - 2), SUB), :], state[pl.ds(at + 2, SUB), :]
                        )
                    near, far = upstream(f, t, at)
                    moved = (v * c0 + source) + (x1 * one + x2 * two) + (y1 * near + y2 * far)
                    out[block(at), :] = moved
                    values.append(moved)
                if not last:
                    sums = add_columns(yw[4 * kg], values[0], values[1], sums)
            if not last:
                totals = add_group(vx, sums, totals)
        if not last:
            put_sums(sums_ref, y, totals)

    def ghost(d, f, t):
        return ghosts[sz.mirror_index(d, f, t)]

    advance(0, lambda f, t, at: (ghost(0, f, t), ghost(1, f, t)))
    advance(1, lambda f, t, at: (state[block(at - SUB), :], ghost(0, f, t)))

    def body(step, carry):
        advance(step, lambda f, t, at: (state[block(at - SUB), :], state[block(at - 2 * SUB), :]))
        return carry

    lax.fori_loop(2, Y, body, 0)
    if not last:
        send(sz, vert_index, out, sums_ref, mirror, packet, right, left)
        return
    for f in range(2):
        for kg in range(sz.kg):
            for xg in range(sz.xg):
                t = xg * sz.kg + kg
                slot = xg % 2
                base = sz.base(f, t)
                for step in range(Y):
                    y = real_row(parity, step)
                    turn[slot, block(y * SUB), :] = out[pl.ds(base + step * SUB, SUB), :]
                parts = []
                for x in range(SUB):
                    for part in range(0, Y, SUB):
                        parts.append(turn[slot, pl.ds(part * SUB + x, SUB, stride=SUB), :])
                turned = jnp.concatenate(parts, axis=0).T
                for k in range(kg * PART_K, min((kg + 1) * PART_K, sz.band)):
                    row = (k - kg * PART_K) * PART_X
                    final[f, k, xg * PART_X : (xg + 1) * PART_X, :] = turned[row : row + PART_X, :]
            chunk_copy(sz, final, result, sems, f, kg).start()
    for f in range(2):
        for kg in range(sz.kg):
            chunk_copy(sz, final, result, sems, f, kg).wait()


def shapes(sz):
    f32 = jnp.float32
    side = jax.ShapeDtypeStruct((sz.side_rows, LANES), f32)
    return (
        jax.ShapeDtypeStruct((sz.state_rows, LANES), f32),
        jax.ShapeDtypeStruct((sz.mirror_blocks + 2, SUB, LANES), f32),
        jax.ShapeDtypeStruct((ROWS, sz.cells), f32),
        side,
        side,
    )


def on_device(distribution, wall_type, wall_temp_index, wall_temps, accommodation):
    _, band, nx, cells = distribution.shape
    vert = lax.axis_size("vert")
    columns = lax.axis_size("gx")
    sz = Sizes(band, nx, cells, vert)
    vmem = pl.BlockSpec(memory_space=pltpu.VMEM)
    smem = pl.BlockSpec(memory_space=pltpu.SMEM)
    hbm = pl.BlockSpec(memory_space=pltpu.HBM)
    final_shape = jax.ShapeDtypeStruct(distribution.shape, jnp.float32)
    bytes_moved = 2 * distribution.size * 4
    sums_scratch = pltpu.VMEM((FIELDS, sz.cells, LANES), jnp.float32)
    turn_scratch = pltpu.VMEM((2, sz.cells, LANES), jnp.float32)
    step_scratch = [
        pltpu.VMEM((FIELDS, sz.cells, LANES), jnp.float32),
        pltpu.VMEM((sz.mirror_blocks, SUB, LANES), jnp.float32),
        pltpu.VMEM((4 * sz.xg, SUB, LANES), jnp.float32),
        pltpu.VMEM((4 * sz.kg, SUB, LANES), jnp.float32),
    ]
    first_vmem = ALL_VMEM - 26 * distribution.size
    stage = [
        pltpu.VMEM(distribution.shape, jnp.float32),
        pltpu.SemaphoreType.DMA((2 * sz.kg,)),
    ]
    state, mirror, packet, right, left = pl.pallas_call(
        functools.partial(first_kernel, sz),
        out_shape=shapes(sz),
        in_specs=[hbm],
        out_specs=(vmem,) * 5,
        scratch_shapes=[sums_scratch, turn_scratch] + stage,
        cost_estimate=pl.CostEstimate(
            flops=10 * distribution.size, bytes_accessed=bytes_moved, transcendentals=0
        ),
        compiler_params=pltpu.CompilerParams(vmem_limit_bytes=first_vmem),
        name="first",
    )(distribution)
    wall = pl.pallas_call(
        functools.partial(wall_kernel, sz),
        out_shape=jax.ShapeDtypeStruct((3, SUB, LANES), jnp.float32),
        in_specs=[smem] * 4,
        out_specs=vmem,
        compiler_params=pltpu.CompilerParams(vmem_limit_bytes=KERNEL_VMEM),
        name="walls",
    )(wall_type, wall_temp_index, wall_temps, accommodation)
    ring = [(i, (i + 1) % columns) for i in range(columns)]
    back = [(j, i) for i, j in ring]
    for iteration in range(ITERS):
        last = iteration == ITERS - 1
        mirror_in = lax.ppermute(mirror, "vert", [(s, s ^ 1) for s in range(vert)])
        right_in = lax.ppermute(right, "gx", ring)
        left_in = lax.ppermute(left, "gx", back)
        others = []
        for mask in range(vert - 1, 1, -1):
            others.append(lax.ppermute(packet, "vert", [(s, s ^ mask) for s in range(vert)]))
        if last:
            scratch = step_scratch + [pltpu.VMEM((sz.state_rows, LANES), jnp.float32), turn_scratch] + stage
        else:
            scratch = step_scratch + [sums_scratch]
        result = pl.pallas_call(
            functools.partial(step_kernel, sz, last),
            out_shape=(final_shape,) if last else shapes(sz),
            in_specs=[vmem] * (6 + len(others)),
            out_specs=(hbm,) if last else (vmem,) * 5,
            scratch_shapes=scratch,
            cost_estimate=pl.CostEstimate(
                flops=40 * distribution.size, bytes_accessed=bytes_moved, transcendentals=0
            ),
            compiler_params=pltpu.CompilerParams(vmem_limit_bytes=KERNEL_VMEM),
            name="last" if last else "step",
        )(state, mirror_in, right_in, left_in, packet, wall, *others)
        if last:
            (state,) = result
        else:
            state, mirror, packet, right, left = result
    return state


def solution(mesh):
    placed = (P(None, "vert", None, "gx"), P(None, "gx"), P(None, "gx"), P(), P())
    return jax.shard_map(
        on_device,
        mesh=mesh,
        in_specs=placed,
        out_specs=P(None, "vert", None, "gx"),
        check_vma=False,
    )
```

```python
import functools
import math

import jax
import jax.numpy as jnp
from jax import lax
from jax.experimental import pallas as pl
from jax.experimental.pallas import tpu as pltpu
from jax.sharding import PartitionSpec as P


Y = 16
ITERS = 4
NTEMP = 2
NTYPE = 3
SUB = 8
LANES = 128
ROWS = 16
PART_X = 16
PART_K = LANES // PART_X
FIELDS = 9
KERNEL_VMEM = 16 * 1024 * 1024
ALL_VMEM = 64 * 1024 * 1024

vmax_speed = 4.5
courant = 0.5
diffusivity_ratio = 2.0 / 3.0
relaxation_multiplier = 2.5
shear_exponent = 0.19
time_increment = courant / vmax_speed


class Sizes:
    def __init__(self, band, nx, cells, vert):
        assert cells == SUB * Y and nx % (2 * PART_X) == 0
        self.band, self.nx, self.cells, self.vert = band, nx, cells, vert
        self.nv = band * vert
        self.xg = nx // PART_X
        self.kg = -(-band // PART_K)
        self.tiles = self.xg * self.kg
        self.half = self.tiles // 2
        self.state_rows = 2 * self.tiles * cells
        self.side_rows = 2 * self.half * Y * 2 + 2 * SUB
        self.mirror_blocks = 4 * self.tiles
        self.weight = 2.0 * vmax_speed / nx * (2.0 * vmax_speed / self.nv)

    def base(self, f, t):
        return (f * self.tiles + t) * self.cells

    def side_base(self, f, t):
        return SUB + (f * self.half + t % self.half) * 2 * Y

    def mirror_index(self, d, f, t):
        return (d * 2 + f) * self.tiles + t


def node_speed(index, number):
    return vmax_speed * (2.0 * index.astype(jnp.float32) + 1.0 - number) / number


def row_speed(sz, vert_index, offset):
    lower = vert_index // 2 * sz.band + offset
    return node_speed(jnp.where(vert_index % 2 == 0, lower, sz.nv - 1 - lower), sz.nv)


def beam_weights(speed):
    s = jnp.abs(speed) * time_increment
    return -1.5 * s + 0.5 * s * s, 2.0 * s - s * s, -0.5 * s + 0.5 * s * s


def lane():
    return lax.broadcasted_iota(jnp.int32, (SUB, LANES), 1)


def sub():
    return lax.broadcasted_iota(jnp.int32, (SUB, LANES), 0)


def x_speed(sz, group):
    return node_speed(group * PART_X + lane() % PART_X, sz.nx)


def y_speed(sz, vert_index, group):
    return row_speed(sz, vert_index, group * PART_K + lane() // PART_X)


def inside(sz, group):
    if (group + 1) * PART_K <= sz.band:
        return None
    return group * PART_K + lane() // PART_X < sz.band


def masked(mask, value):
    return value if mask is None else jnp.where(mask, value, 0.0)


def real_row(parity, step):
    return jnp.where(parity == 0, Y - 1 - step, step)


def block(start):
    return pl.ds(pl.multiple_of(start, SUB), SUB)


def add_columns(vy, g, h, sums):
    p = vy * g
    q = vy * p
    r = vy * (q + h)
    new = (g, p, q, r, h)
    return new if sums is None else tuple(a + b for a, b in zip(sums, new))


def add_group(vx, sums, totals):
    t0, t1, t2, t3, u0 = sums
    a = vx * t0
    b = vx * a
    c = vx * t1
    new = (t0, a, t1, b, c, t2, u0, vx * (b + t2 + u0), vx * c + t3)
    return new if totals is None else tuple(x + y for x, y in zip(totals, new))


def put_sums(sums_ref, y, totals):
    for m, total in enumerate(totals):
        sums_ref[m, block(y * SUB), :] = total


def send(sz, vert_index, state, sums_ref, mirror, packet, right, left):
    rows = []
    for m in range(FIELDS):
        rows.append(jnp.sum(sums_ref[m].T, axis=0, keepdims=True) * sz.weight)
    n, mx, my, pxx, pxy, pyy, extra, tx, ty = rows
    even = vert_index % 2 == 0
    zero = jnp.zeros_like(n)
    rows = [n, mx, my, pxx + pyy + extra, pxx, pxy, pyy, tx, ty]
    rows += [jnp.where(even, -my, zero), jnp.where(even, zero, my)]
    rows += [zero] * (ROWS - len(rows))
    for r, value in enumerate(rows):
        packet[r : r + 1, :] = value
        mirror[sz.mirror_blocks + r // SUB, r % SUB : r % SUB + 1, :] = value
    for f in range(2):
        for t in range(sz.tiles):
            base = sz.base(f, t)
            for d in range(2):
                mirror[sz.mirror_index(d, f, t)] = state[pl.ds(base + (Y - 1 - d) * SUB, SUB), :]
            positive = t >= sz.half
            out = right if positive else left
            side = sz.side_base(f, t)
            _, x1, x2 = beam_weights(x_speed(sz, t // sz.kg))
            ends = (SUB - 1, SUB - 2) if positive else (0, 1)
            for part in range(0, Y, SUB):
                near, far = [
                    state[pl.ds(base + part * SUB + c, SUB, stride=SUB), :] for c in ends
                ]
                pair = (x1 * near + x2 * far, x2 * near)
                for c in range(2):
                    value = pair[c] if positive else pair[1 - c]
                    out[pl.ds(side + 2 * part + c, SUB, stride=2), :] = value
    pad = jnp.zeros((SUB, LANES), jnp.float32)
    for out in (right, left):
        out[0:SUB, :] = pad
        out[sz.side_rows - SUB : sz.side_rows, :] = pad


def wall_kernel(sz, type_ref, index_ref, temps_ref, acc_ref, wall, xw, yw, emission):
    face = 1 - lax.axis_index("vert") % 2
    column = sub()
    kind = jnp.zeros_like(column)
    entry = jnp.zeros_like(column)
    for x in range(SUB):
        kind = jnp.where(column == x, type_ref[face, x], kind)
        entry = jnp.where(column == x, index_ref[face, x], entry)
    percent = jnp.zeros_like(column)
    for t in range(NTYPE):
        percent = jnp.where(kind == t, acc_ref[t], percent)
    alpha = percent.astype(jnp.float32) / 100.0
    heat = jnp.ones((SUB, LANES), jnp.float32)
    denom = jnp.ones((SUB, LANES), jnp.float32)

    def grid(number):
        index = lax.broadcasted_iota(jnp.int32, (1, -(-number // LANES) * LANES), 1)
        return node_speed(index, number), index < number

    vx, in_x = grid(sz.nx)
    vy, in_y = grid(sz.nv)
    for t in range(NTEMP):
        temp = jnp.full((1, 1), temps_ref[t], jnp.float32)
        along = jnp.sum(jnp.where(in_x, jnp.exp(-vx * vx / temp), 0.0), axis=1, keepdims=True)
        across = jnp.sum(
            jnp.where(in_y, jnp.maximum(vy, 0.0) * jnp.exp(-vy * vy / temp), 0.0),
            axis=1,
            keepdims=True,
        )
        inward = sz.weight * along * across / (math.pi * temp)
        heat = jnp.where(entry == t, temp, heat)
        denom = jnp.where(entry == t, inward, denom)
    wall[0] = 1.0 - alpha
    emitted = alpha / (denom * (math.pi * heat))
    vert_index = lax.axis_index("vert")
    inv_heat = 1.0 / heat
    wall_y = []
    for kg in range(sz.kg):
        vy = y_speed(sz, vert_index, kg)
        for r, value in enumerate((vy,) + beam_weights(vy)):
            yw[4 * kg + r] = value
        wall_y.append(masked(inside(sz, kg), emitted * jnp.exp(-vy * vy * inv_heat)))
    for xg in range(sz.xg):
        vx = x_speed(sz, xg)
        for r, value in enumerate((vx,) + beam_weights(vx)):
            xw[4 * xg + r] = value
        wall_x = jnp.exp(-vx * vx * inv_heat)
        for kg in range(sz.kg):
            diffuse = wall_x * wall_y[kg]
            emission[xg * sz.kg + kg] = diffuse
            emission[sz.tiles + xg * sz.kg + kg] = 0.5 * heat * diffuse


def chunk_copy(sz, source, target, sems, f, kg):
    rows = pl.ds(kg * PART_K, min(PART_K, sz.band - kg * PART_K))
    return pltpu.make_async_copy(
        source.at[f, rows], target.at[f, rows], sems.at[f * sz.kg + kg]
    )


def first_kernel(sz, argument, state, mirror, packet, right, left, sums_ref, turn, given, sems):
    vert_index = lax.axis_index("vert")
    parity = vert_index % 2
    for f in range(2):
        for kg in range(sz.kg):
            chunk_copy(sz, argument, given, sems, f, kg).start()
    for f in range(2):
        for kg in range(sz.kg):
            chunk_copy(sz, argument, given, sems, f, kg).wait()
            for xg in range(sz.xg):
                parts = []
                for k in range(kg * PART_K, (kg + 1) * PART_K):
                    if k < sz.band:
                        parts.append(given[f, k, xg * PART_X : (xg + 1) * PART_X, :])
                    else:
                        parts.append(jnp.zeros((PART_X, sz.cells), jnp.float32))
                turned = jnp.concatenate(parts, axis=0).T
                t = xg * sz.kg + kg
                slot = xg % 2
                for x in range(SUB):
                    for part in range(0, Y, SUB):
                        piece = turned[x * Y + part : x * Y + part + SUB, :]
                        turn[slot, pl.ds(part * SUB + x, SUB, stride=SUB), :] = piece
                base = sz.base(f, t)
                for step in range(Y):
                    y = real_row(parity, step)
                    state[pl.ds(base + step * SUB, SUB), :] = turn[slot, block(y * SUB), :]

    def step_body(step, carry):
        totals = None
        for xg in range(sz.xg):
            sums = None
            for kg in range(sz.kg):
                g, h = [state[block(sz.base(f, xg * sz.kg + kg) + step * SUB), :] for f in range(2)]
                sums = add_columns(y_speed(sz, vert_index, kg), g, h, sums)
            totals = add_group(x_speed(sz, xg), sums, totals)
        put_sums(sums_ref, real_row(parity, step), totals)
        return carry

    lax.fori_loop(0, Y, step_body, 0)
    send(sz, vert_index, state, sums_ref, mirror, packet, right, left)


def fields_of(parity, tot):
    def row(r):
        return tot[r // SUB][r % SUB : r % SUB + 1, :]

    n, mx, my, energy, pxx, pxy, pyy, tx, ty = [row(r) for r in range(9)]
    inv_n = 1.0 / n
    ux, uy = mx * inv_n, my * inv_n
    usq = ux * ux + uy * uy
    theta = 2.0 / 3.0 * (energy * inv_n - usq)
    along = ux * mx + uy * my
    qx = tx - 2.0 * (ux * pxx + uy * pxy) + usq * mx - ux * energy + 2.0 * ux * along - ux * usq * n
    qy = ty - 2.0 * (ux * pxy + uy * pyy) + usq * my - uy * energy + 2.0 * uy * along - uy * usq * n
    inv_t = 1.0 / theta
    rate = (time_increment * relaxation_multiplier) * n * jnp.exp(shear_exponent * jnp.log(theta))
    amount = rate * n * inv_t * (1.0 / math.pi)
    scale = (1.0 - diffusivity_ratio) * 0.8 * inv_n * inv_t * inv_t
    flux = jnp.where(parity == 0, row(10), row(9))
    return [ux, uy, inv_t, amount, scale * qx, scale * qy, 0.5 * theta, rate, flux]


def advect_kernel(sz, state, xw, yw, out):
    column = sub()

    def advance(step, near_at, far_at):
        for xg in range(sz.xg):
            x0 = 1.0 + xw[4 * xg + 1]
            x1, x2 = xw[4 * xg + 2], xw[4 * xg + 3]
            for kg in range(sz.kg):
                t = xg * sz.kg + kg
                c0 = x0 + yw[4 * kg + 1]
                y1, y2 = yw[4 * kg + 2], yw[4 * kg + 3]
                for f in range(2):
                    at = sz.base(f, t) + step * SUB
                    v = state[block(at), :]
                    if t >= sz.half:
                        one = jnp.where(column < 1, 0.0, state[pl.ds(at - 1, SUB), :])
                        two = jnp.where(column < 2, 0.0, state[pl.ds(at - 2, SUB), :])
                    else:
                        one = jnp.where(column >= SUB - 1, 0.0, state[pl.ds(at + 1, SUB), :])
                        two = jnp.where(column >= SUB - 2, 0.0, state[pl.ds(at + 2, SUB), :])
                    moved = v * c0 + (x1 * one + x2 * two)
                    if near_at:
                        moved = moved + y1 * state[block(at - SUB), :]
                    if far_at:
                        moved = moved + y2 * state[block(at - 2 * SUB), :]
                    out[block(at), :] = moved

    advance(0, False, False)
    advance(1, True, False)

    def body(step, carry):
        advance(step, True, True)
        return carry

    lax.fori_loop(2, Y, body, 0)


def spread_fields(sz, rows, spread):
    index = lax.broadcasted_iota(jnp.int32, (ROWS, LANES), 0)
    table = jnp.zeros((ROWS, sz.cells), jnp.float32)
    for r, value in enumerate(rows):
        table = jnp.where(index == r, value, table)
    parts = []
    for _ in range(3):
        part = table.astype(jnp.bfloat16)
        parts.append(part)
        table = table - part.astype(jnp.float32)
    parts = jnp.concatenate(parts, axis=0)
    index = lax.broadcasted_iota(jnp.int32, (3 * ROWS, LANES), 0) % ROWS
    picks = [(index == r).astype(jnp.float32).astype(jnp.bfloat16) for r in range(FIELDS)]
    wide = lax.dot_general(
        parts, jnp.concatenate(picks, axis=1), (((0,), (0,)), ((), ())),
        preferred_element_type=jnp.float32,
    )
    for r in range(FIELDS):
        spread[r] = wide[:, r * LANES : (r + 1) * LANES]


def step_kernel(sz, last, *refs):
    refs = list(refs)
    state, inner, mirror_in, right_in, left_in, packet_in, wall, xw, yw, emission = refs[:10]
    others = refs[10 : 10 + sz.vert - 2]
    rest = refs[10 + sz.vert - 2 :]
    if last:
        (result, spread, out, turn, final, sems) = rest
    else:
        (out, mirror, packet, right, left, spread, sums_ref) = rest
    vert_index = lax.axis_index("vert")
    parity = vert_index % 2

    tot = [packet_in[SUB * b : SUB * b + SUB, :] + mirror_in[sz.mirror_blocks + b] for b in range(2)]
    for other in others:
        tot = [tot[b] + other[SUB * b : SUB * b + SUB, :] for b in range(2)]
    spread_fields(sz, fields_of(parity, tot), spread)

    keep = wall[0]
    flux = spread[FIELDS - 1, block(real_row(parity, 0) * SUB), :]
    column = sub()

    def ghost(d, f, t):
        return keep * mirror_in[sz.mirror_index(d, f, t)] + flux * emission[f * sz.tiles + t]

    def advance(step, beyond):
        y = real_row(parity, step)
        ux, uy, inv_t, amount, px, py, half_theta, rate = [
            spread[r, block(y * SUB), :] for r in range(FIELDS - 1)
        ]
        along_y = []
        for kg in range(sz.kg):
            cy = yw[4 * kg] - uy
            cy_sq = cy * cy * inv_t
            along_y.append((masked(inside(sz, kg), amount * jnp.exp(-cy_sq)), py * cy, cy_sq - 2.0))
        totals = None
        for xg in range(sz.xg):
            vx = xw[4 * xg]
            cx = vx - ux
            cx_sq = cx * cx * inv_t
            ex = jnp.exp(-cx_sq)
            pxs = px * cx
            sums = None
            for kg in range(sz.kg):
                t = xg * sz.kg + kg
                ey, pys, cys = along_y[kg]
                maxwell = ex * ey
                p = pxs + pys
                sg = maxwell * (1.0 + p * (cx_sq + cys))
                sh = half_theta * (sg + p * maxwell)
                values = []
                for f, source in ((0, sg), (1, sh)):
                    at = sz.base(f, t) + step * SUB
                    side = sz.side_base(f, t) + 2 * step
                    if t >= sz.half:
                        edge = jnp.where(column < 2, right_in[pl.ds(side, SUB), :], 0.0)
                    else:
                        start = side - (SUB - 2)
                        edge = jnp.where(column >= SUB - 2, left_in[pl.ds(start, SUB), :], 0.0)
                    moved = (inner[block(at), :] + edge) + (source - rate * state[block(at), :])
                    if beyond is not None:
                        moved = moved + beyond(f, t, yw[4 * kg + 2], yw[4 * kg + 3])
                    out[block(at), :] = moved
                    values.append(moved)
                if not last:
                    sums = add_columns(yw[4 * kg], values[0], values[1], sums)
            if not last:
                totals = add_group(vx, sums, totals)
        if not last:
            put_sums(sums_ref, y, totals)

    advance(0, lambda f, t, y1, y2: y1 * ghost(0, f, t) + y2 * ghost(1, f, t))
    advance(1, lambda f, t, y1, y2: y2 * ghost(0, f, t))

    def body(step, carry):
        advance(step, None)
        return carry

    lax.fori_loop(2, Y, body, 0)
    if not last:
        send(sz, vert_index, out, sums_ref, mirror, packet, right, left)
        return
    for f in range(2):
        for kg in range(sz.kg):
            for xg in range(sz.xg):
                t = xg * sz.kg + kg
                slot = xg % 2
                base = sz.base(f, t)
                for step in range(Y):
                    y = real_row(parity, step)
                    turn[slot, block(y * SUB), :] = out[pl.ds(base + step * SUB, SUB), :]
                parts = []
                for x in range(SUB):
                    for part in range(0, Y, SUB):
                        parts.append(turn[slot, pl.ds(part * SUB + x, SUB, stride=SUB), :])
                turned = jnp.concatenate(parts, axis=0).T
                for k in range(kg * PART_K, min((kg + 1) * PART_K, sz.band)):
                    row = (k - kg * PART_K) * PART_X
                    final[f, k, xg * PART_X : (xg + 1) * PART_X, :] = turned[row : row + PART_X, :]
            chunk_copy(sz, final, result, sems, f, kg).start()
    for f in range(2):
        for kg in range(sz.kg):
            chunk_copy(sz, final, result, sems, f, kg).wait()


def shapes(sz):
    f32 = jnp.float32
    side = jax.ShapeDtypeStruct((sz.side_rows, LANES), f32)
    return (
        jax.ShapeDtypeStruct((sz.state_rows, LANES), f32),
        jax.ShapeDtypeStruct((sz.mirror_blocks + 2, SUB, LANES), f32),
        jax.ShapeDtypeStruct((ROWS, sz.cells), f32),
        side,
        side,
    )


def on_device(distribution, wall_type, wall_temp_index, wall_temps, accommodation):
    _, band, nx, cells = distribution.shape
    vert = lax.axis_size("vert")
    columns = lax.axis_size("gx")
    sz = Sizes(band, nx, cells, vert)
    vmem = pl.BlockSpec(memory_space=pltpu.VMEM)
    smem = pl.BlockSpec(memory_space=pltpu.SMEM)
    hbm = pl.BlockSpec(memory_space=pltpu.HBM)
    final_shape = jax.ShapeDtypeStruct(distribution.shape, jnp.float32)
    bytes_moved = 2 * distribution.size * 4
    sums_scratch = pltpu.VMEM((FIELDS, sz.cells, LANES), jnp.float32)
    turn_scratch = pltpu.VMEM((2, sz.cells, LANES), jnp.float32)
    step_scratch = [pltpu.VMEM((FIELDS, sz.cells, LANES), jnp.float32)]
    first_vmem = ALL_VMEM - 26 * distribution.size
    stage = [
        pltpu.VMEM(distribution.shape, jnp.float32),
        pltpu.SemaphoreType.DMA((2 * sz.kg,)),
    ]
    state, mirror, packet, right, left = pl.pallas_call(
        functools.partial(first_kernel, sz),
        out_shape=shapes(sz),
        in_specs=[hbm],
        out_specs=(vmem,) * 5,
        scratch_shapes=[sums_scratch, turn_scratch] + stage,
        cost_estimate=pl.CostEstimate(
            flops=10 * distribution.size, bytes_accessed=bytes_moved, transcendentals=0
        ),
        compiler_params=pltpu.CompilerParams(vmem_limit_bytes=first_vmem),
        name="first",
    )(distribution)
    tables = pl.pallas_call(
        functools.partial(wall_kernel, sz),
        out_shape=tuple(
            jax.ShapeDtypeStruct((count, SUB, LANES), jnp.float32)
            for count in (1, 4 * sz.xg, 4 * sz.kg, 2 * sz.tiles)
        ),
        in_specs=[smem] * 4,
        out_specs=(vmem,) * 4,
        compiler_params=pltpu.CompilerParams(vmem_limit_bytes=KERNEL_VMEM),
        name="walls",
    )(wall_type, wall_temp_index, wall_temps, accommodation)
    ring = [(i, (i + 1) % columns) for i in range(columns)]
    back = [(j, i) for i, j in ring]
    for iteration in range(ITERS):
        last = iteration == ITERS - 1
        mirror_in = lax.ppermute(mirror, "vert", [(s, s ^ 1) for s in range(vert)])
        right_in = lax.ppermute(right, "gx", ring)
        left_in = lax.ppermute(left, "gx", back)
        others = []
        for mask in range(vert - 1, 1, -1):
            others.append(lax.ppermute(packet, "vert", [(s, s ^ mask) for s in range(vert)]))
        inner = pl.pallas_call(
            functools.partial(advect_kernel, sz),
            out_shape=jax.ShapeDtypeStruct((sz.state_rows, LANES), jnp.float32),
            in_specs=[vmem] * 3,
            out_specs=vmem,
            cost_estimate=pl.CostEstimate(
                flops=12 * distribution.size, bytes_accessed=bytes_moved, transcendentals=0
            ),
            compiler_params=pltpu.CompilerParams(vmem_limit_bytes=KERNEL_VMEM),
            name="advect",
        )(state, tables[1], tables[2])
        if last:
            scratch = step_scratch + [pltpu.VMEM((sz.state_rows, LANES), jnp.float32), turn_scratch] + stage
        else:
            scratch = step_scratch + [sums_scratch]
        result = pl.pallas_call(
            functools.partial(step_kernel, sz, last),
            out_shape=(final_shape,) if last else shapes(sz),
            in_specs=[vmem] * (10 + len(others)),
            out_specs=(hbm,) if last else (vmem,) * 5,
            scratch_shapes=scratch,
            cost_estimate=pl.CostEstimate(
                flops=40 * distribution.size, bytes_accessed=bytes_moved, transcendentals=0
            ),
            compiler_params=pltpu.CompilerParams(vmem_limit_bytes=KERNEL_VMEM),
            name="last" if last else "step",
        )(state, inner, mirror_in, right_in, left_in, packet, *tables, *others)
        if last:
            (state,) = result
        else:
            state, mirror, packet, right, left = result
    return state


def solution(mesh):
    placed = (P(None, "vert", None, "gx"), P(None, "gx"), P(None, "gx"), P(), P())
    return jax.shard_map(
        on_device,
        mesh=mesh,
        in_specs=placed,
        out_specs=P(None, "vert", None, "gx"),
        check_vma=False,
    )
```

```python
import functools
import math

import jax
import jax.numpy as jnp
from jax import lax
from jax.experimental import pallas as pl
from jax.experimental.pallas import tpu as pltpu
from jax.sharding import PartitionSpec as P


Y = 16
ITERS = 4
NTEMP = 2
NTYPE = 3
SUB = 8
LANES = 128
ROWS = 16
PART_X = 16
PART_K = LANES // PART_X
FIELDS = 9
KERNEL_VMEM = 16 * 1024 * 1024
ALL_VMEM = 64 * 1024 * 1024

vmax_speed = 4.5
courant = 0.5
diffusivity_ratio = 2.0 / 3.0
relaxation_multiplier = 2.5
shear_exponent = 0.19
time_increment = courant / vmax_speed


class Sizes:
    def __init__(self, band, nx, cells, vert):
        assert cells == SUB * Y and nx % (2 * PART_X) == 0
        self.band, self.nx, self.cells, self.vert = band, nx, cells, vert
        self.nv = band * vert
        self.xg = nx // PART_X
        self.kg = -(-band // PART_K)
        self.tiles = self.xg * self.kg
        self.half = self.tiles // 2
        self.state_rows = 2 * self.tiles * cells
        self.side_rows = 2 * self.half * Y * 2 + 2 * SUB
        self.mirror_blocks = 4 * self.tiles
        self.weight = 2.0 * vmax_speed / nx * (2.0 * vmax_speed / self.nv)

    def base(self, f, t):
        return (f * self.tiles + t) * self.cells

    def side_base(self, f, t):
        return SUB + (f * self.half + t % self.half) * 2 * Y

    def mirror_index(self, d, f, t):
        return (d * 2 + f) * self.tiles + t


def node_speed(index, number):
    return vmax_speed * (2.0 * index.astype(jnp.float32) + 1.0 - number) / number


def row_speed(sz, vert_index, offset):
    lower = vert_index // 2 * sz.band + offset
    return node_speed(jnp.where(vert_index % 2 == 0, lower, sz.nv - 1 - lower), sz.nv)


def beam_weights(speed):
    s = jnp.abs(speed) * time_increment
    return -1.5 * s + 0.5 * s * s, 2.0 * s - s * s, -0.5 * s + 0.5 * s * s


def lane():
    return lax.broadcasted_iota(jnp.int32, (SUB, LANES), 1)


def sub():
    return lax.broadcasted_iota(jnp.int32, (SUB, LANES), 0)


def x_speed(sz, group):
    return node_speed(group * PART_X + lane() % PART_X, sz.nx)


def y_speed(sz, vert_index, group):
    return row_speed(sz, vert_index, group * PART_K + lane() // PART_X)


def inside(sz, group):
    if (group + 1) * PART_K <= sz.band:
        return None
    return group * PART_K + lane() // PART_X < sz.band


def masked(mask, value):
    return value if mask is None else jnp.where(mask, value, 0.0)


def real_row(parity, step):
    return jnp.where(parity == 0, Y - 1 - step, step)


def block(start):
    return pl.ds(pl.multiple_of(start, SUB), SUB)


def add_columns(vy, g, h, sums):
    p = vy * g
    q = vy * p
    r = vy * (q + h)
    new = (g, p, q, r, h)
    return new if sums is None else tuple(a + b for a, b in zip(sums, new))


def add_group(vx, sums, totals):
    t0, t1, t2, t3, u0 = sums
    a = vx * t0
    b = vx * a
    c = vx * t1
    new = (t0, a, t1, b, c, t2, u0, vx * (b + t2 + u0), vx * c + t3)
    return new if totals is None else tuple(x + y for x, y in zip(totals, new))


def put_sums(sums_ref, y, totals):
    for m, total in enumerate(totals):
        sums_ref[m, block(y * SUB), :] = total


def send(sz, vert_index, state, sums_ref, mirror, packet, right, left):
    rows = []
    for m in range(FIELDS):
        rows.append(jnp.sum(sums_ref[m].T, axis=0, keepdims=True) * sz.weight)
    n, mx, my, pxx, pxy, pyy, extra, tx, ty = rows
    even = vert_index % 2 == 0
    zero = jnp.zeros_like(n)
    rows = [n, mx, my, pxx + pyy + extra, pxx, pxy, pyy, tx, ty]
    rows += [jnp.where(even, -my, zero), jnp.where(even, zero, my)]
    rows += [zero] * (ROWS - len(rows))
    for r, value in enumerate(rows):
        packet[r : r + 1, :] = value
        mirror[sz.mirror_blocks + r // SUB, r % SUB : r % SUB + 1, :] = value
    for f in range(2):
        for t in range(sz.tiles):
            base = sz.base(f, t)
            for d in range(2):
                mirror[sz.mirror_index(d, f, t)] = state[pl.ds(base + (Y - 1 - d) * SUB, SUB), :]
            positive = t >= sz.half
            out = right if positive else left
            side = sz.side_base(f, t)
            _, x1, x2 = beam_weights(x_speed(sz, t // sz.kg))
            ends = (SUB - 1, SUB - 2) if positive else (0, 1)
            for part in range(0, Y, SUB):
                near, far = [
                    state[pl.ds(base + part * SUB + c, SUB, stride=SUB), :] for c in ends
                ]
                pair = (x1 * near + x2 * far, x2 * near)
                for c in range(2):
                    value = pair[c] if positive else pair[1 - c]
                    out[pl.ds(side + 2 * part + c, SUB, stride=2), :] = value
    pad = jnp.zeros((SUB, LANES), jnp.float32)
    for out in (right, left):
        out[0:SUB, :] = pad
        out[sz.side_rows - SUB : sz.side_rows, :] = pad


def wall_kernel(sz, type_ref, index_ref, temps_ref, acc_ref, wall, xw, yw, emission):
    face = 1 - lax.axis_index("vert") % 2
    column = sub()
    kind = jnp.zeros_like(column)
    entry = jnp.zeros_like(column)
    for x in range(SUB):
        kind = jnp.where(column == x, type_ref[face, x], kind)
        entry = jnp.where(column == x, index_ref[face, x], entry)
    percent = jnp.zeros_like(column)
    for t in range(NTYPE):
        percent = jnp.where(kind == t, acc_ref[t], percent)
    alpha = percent.astype(jnp.float32) / 100.0
    heat = jnp.ones((SUB, LANES), jnp.float32)
    denom = jnp.ones((SUB, LANES), jnp.float32)

    def grid(number):
        index = lax.broadcasted_iota(jnp.int32, (1, -(-number // LANES) * LANES), 1)
        return node_speed(index, number), index < number

    vx, in_x = grid(sz.nx)
    vy, in_y = grid(sz.nv)
    for t in range(NTEMP):
        temp = jnp.full((1, 1), temps_ref[t], jnp.float32)
        along = jnp.sum(jnp.where(in_x, jnp.exp(-vx * vx / temp), 0.0), axis=1, keepdims=True)
        across = jnp.sum(
            jnp.where(in_y, jnp.maximum(vy, 0.0) * jnp.exp(-vy * vy / temp), 0.0),
            axis=1,
            keepdims=True,
        )
        inward = sz.weight * along * across / (math.pi * temp)
        heat = jnp.where(entry == t, temp, heat)
        denom = jnp.where(entry == t, inward, denom)
    wall[0] = 1.0 - alpha
    emitted = alpha / (denom * (math.pi * heat))
    vert_index = lax.axis_index("vert")
    inv_heat = 1.0 / heat
    wall_y = []
    for kg in range(sz.kg):
        vy = y_speed(sz, vert_index, kg)
        for r, value in enumerate((vy,) + beam_weights(vy)):
            yw[4 * kg + r] = value
        wall_y.append(masked(inside(sz, kg), emitted * jnp.exp(-vy * vy * inv_heat)))
    for xg in range(sz.xg):
        vx = x_speed(sz, xg)
        for r, value in enumerate((vx,) + beam_weights(vx)):
            xw[4 * xg + r] = value
        wall_x = jnp.exp(-vx * vx * inv_heat)
        for kg in range(sz.kg):
            diffuse = wall_x * wall_y[kg]
            emission[xg * sz.kg + kg] = diffuse
            emission[sz.tiles + xg * sz.kg + kg] = 0.5 * heat * diffuse


def group_copy(sz, source, target, sems, f, xg):
    speeds = pl.ds(xg * PART_X, PART_X)
    return pltpu.make_async_copy(
        source.at[f, :, speeds], target.at[f, :, speeds], sems.at[f * sz.xg + xg]
    )


def first_kernel(sz, argument, state, mirror, packet, right, left, sums_ref, turn_a, turn_b, given, sems):
    vert_index = lax.axis_index("vert")
    parity = vert_index % 2
    for xg in range(sz.xg):
        for f in range(2):
            group_copy(sz, argument, given, sems, f, xg).start()
    for xg in range(sz.xg):
        turn = turn_b if xg % 2 else turn_a
        for f in range(2):
            group_copy(sz, argument, given, sems, f, xg).wait()
        for kg in range(sz.kg):
            for f in range(2):
                parts = []
                for k in range(kg * PART_K, (kg + 1) * PART_K):
                    if k < sz.band:
                        parts.append(given[f, k, xg * PART_X : (xg + 1) * PART_X, :])
                    else:
                        parts.append(jnp.zeros((PART_X, sz.cells), jnp.float32))
                turned = jnp.concatenate(parts, axis=0).T
                slot = 2 * kg + f
                for x in range(SUB):
                    for part in range(0, Y, SUB):
                        piece = turned[x * Y + part : x * Y + part + SUB, :]
                        turn[slot, pl.ds(part * SUB + x, SUB, stride=SUB), :] = piece
        vx = x_speed(sz, xg)
        for step in range(Y):
            y = real_row(parity, step)
            sums = None
            for kg in range(sz.kg):
                g, h = [turn[2 * kg + f, block(y * SUB), :] for f in range(2)]
                for f, value in enumerate((g, h)):
                    state[pl.ds(sz.base(f, xg * sz.kg + kg) + step * SUB, SUB), :] = value
                sums = add_columns(y_speed(sz, vert_index, kg), g, h, sums)
            for m, total in enumerate(add_group(vx, sums, None)):
                if xg:
                    total = total + sums_ref[m, block(y * SUB), :]
                sums_ref[m, block(y * SUB), :] = total
    send(sz, vert_index, state, sums_ref, mirror, packet, right, left)


def fields_of(parity, tot):
    def row(r):
        return tot[r // SUB][r % SUB : r % SUB + 1, :]

    n, mx, my, energy, pxx, pxy, pyy, tx, ty = [row(r) for r in range(9)]
    inv_n = 1.0 / n
    ux, uy = mx * inv_n, my * inv_n
    usq = ux * ux + uy * uy
    theta = 2.0 / 3.0 * (energy * inv_n - usq)
    along = ux * mx + uy * my
    qx = tx - 2.0 * (ux * pxx + uy * pxy) + usq * mx - ux * energy + 2.0 * ux * along - ux * usq * n
    qy = ty - 2.0 * (ux * pxy + uy * pyy) + usq * my - uy * energy + 2.0 * uy * along - uy * usq * n
    inv_t = 1.0 / theta
    rate = (time_increment * relaxation_multiplier) * n * jnp.exp(shear_exponent * jnp.log(theta))
    amount = rate * n * inv_t * (1.0 / math.pi)
    scale = (1.0 - diffusivity_ratio) * 0.8 * inv_n * inv_t * inv_t
    flux = jnp.where(parity == 0, row(10), row(9))
    return [ux, uy, inv_t, amount, scale * qx, scale * qy, 0.5 * theta, rate, flux]


def advect_kernel(sz, state, xw, yw, out):
    column = sub()

    def advance(step, near_at, far_at):
        for xg in range(sz.xg):
            x0 = 1.0 + xw[4 * xg + 1]
            x1, x2 = xw[4 * xg + 2], xw[4 * xg + 3]
            for kg in range(sz.kg):
                t = xg * sz.kg + kg
                c0 = x0 + yw[4 * kg + 1]
                y1, y2 = yw[4 * kg + 2], yw[4 * kg + 3]
                for f in range(2):
                    at = sz.base(f, t) + step * SUB
                    v = state[block(at), :]
                    if t >= sz.half:
                        one = jnp.where(column < 1, 0.0, state[pl.ds(at - 1, SUB), :])
                        two = jnp.where(column < 2, 0.0, state[pl.ds(at - 2, SUB), :])
                    else:
                        one = jnp.where(column >= SUB - 1, 0.0, state[pl.ds(at + 1, SUB), :])
                        two = jnp.where(column >= SUB - 2, 0.0, state[pl.ds(at + 2, SUB), :])
                    moved = v * c0 + (x1 * one + x2 * two)
                    if near_at:
                        moved = moved + y1 * state[block(at - SUB), :]
                    if far_at:
                        moved = moved + y2 * state[block(at - 2 * SUB), :]
                    out[block(at), :] = moved

    advance(0, False, False)
    advance(1, True, False)

    def body(step, carry):
        advance(step, True, True)
        return carry

    lax.fori_loop(2, Y, body, 0)


def spread_fields(sz, rows, spread):
    index = lax.broadcasted_iota(jnp.int32, (ROWS, LANES), 0)
    table = jnp.zeros((ROWS, sz.cells), jnp.float32)
    for r, value in enumerate(rows):
        table = jnp.where(index == r, value, table)
    parts = []
    for _ in range(3):
        part = table.astype(jnp.bfloat16)
        parts.append(part)
        table = table - part.astype(jnp.float32)
    parts = jnp.concatenate(parts, axis=0)
    index = lax.broadcasted_iota(jnp.int32, (3 * ROWS, LANES), 0) % ROWS
    picks = [(index == r).astype(jnp.float32).astype(jnp.bfloat16) for r in range(FIELDS)]
    wide = lax.dot_general(
        parts, jnp.concatenate(picks, axis=1), (((0,), (0,)), ((), ())),
        preferred_element_type=jnp.float32,
    )
    for r in range(FIELDS):
        spread[r] = wide[:, r * LANES : (r + 1) * LANES]


def received(sz, parity, mirror_in, packet_in, others, spread):
    tot = [packet_in[SUB * b : SUB * b + SUB, :] + mirror_in[sz.mirror_blocks + b] for b in range(2)]
    for other in others:
        tot = [tot[b] + other[SUB * b : SUB * b + SUB, :] for b in range(2)]
    spread_fields(sz, fields_of(parity, tot), spread)


def side_edge(sz, right_in, left_in, f, t, step):
    column = sub()
    side = sz.side_base(f, t) + 2 * step
    if t >= sz.half:
        return jnp.where(column < 2, right_in[pl.ds(side, SUB), :], 0.0)
    start = side - (SUB - 2)
    return jnp.where(column >= SUB - 2, left_in[pl.ds(start, SUB), :], 0.0)


def field_rows(spread, y):
    return [spread[r, block(y * SUB), :] for r in range(FIELDS - 1)]


def part_y(sz, yw, kg, uy, inv_t, amount, py):
    cy = yw[4 * kg] - uy
    cy_sq = cy * cy * inv_t
    return masked(inside(sz, kg), amount * jnp.exp(-cy_sq)), py * cy, cy_sq - 2.0


def part_x(vx, ux, inv_t, px):
    cx = vx - ux
    cx_sq = cx * cx * inv_t
    return jnp.exp(-cx_sq), px * cx, cx_sq


def target(along_x, along_y, half_theta):
    ex, pxs, cx_sq = along_x
    ey, pys, cys = along_y
    maxwell = ex * ey
    p = pxs + pys
    sg = maxwell * (1.0 + p * (cx_sq + cys))
    return sg, half_theta * (sg + p * maxwell)


def wall_part(sz, mirror_in, wall, emission, flux, yw):
    def ghost(d, f, t):
        return wall[0] * mirror_in[sz.mirror_index(d, f, t)] + flux * emission[f * sz.tiles + t]

    def beyond(step, f, t):
        kg = t % sz.kg
        y1, y2 = yw[4 * kg + 2], yw[4 * kg + 3]
        if step == 0:
            return y1 * ghost(0, f, t) + y2 * ghost(1, f, t)
        return y2 * ghost(0, f, t)

    return beyond


def step_kernel(sz, *refs):
    state, inner, mirror_in, right_in, left_in, packet_in, wall, xw, yw, emission = refs[:10]
    others = refs[10 : 10 + sz.vert - 2]
    out, mirror, packet, right, left, spread, sums_ref = refs[10 + sz.vert - 2 :]
    vert_index = lax.axis_index("vert")
    parity = vert_index % 2
    received(sz, parity, mirror_in, packet_in, others, spread)
    flux = spread[FIELDS - 1, block(real_row(parity, 0) * SUB), :]
    beyond = wall_part(sz, mirror_in, wall, emission, flux, yw)

    def advance(step, near_wall):
        y = real_row(parity, step)
        ux, uy, inv_t, amount, px, py, half_theta, rate = field_rows(spread, y)
        along_y = [part_y(sz, yw, kg, uy, inv_t, amount, py) for kg in range(sz.kg)]
        totals = None
        for xg in range(sz.xg):
            vx = xw[4 * xg]
            along_x = part_x(vx, ux, inv_t, px)
            sums = None
            for kg in range(sz.kg):
                t = xg * sz.kg + kg
                values = []
                for f, source in enumerate(target(along_x, along_y[kg], half_theta)):
                    at = sz.base(f, t) + step * SUB
                    edge = side_edge(sz, right_in, left_in, f, t, step)
                    moved = (inner[block(at), :] + edge) + (source - rate * state[block(at), :])
                    if near_wall:
                        moved = moved + beyond(step, f, t)
                    out[block(at), :] = moved
                    values.append(moved)
                sums = add_columns(yw[4 * kg], values[0], values[1], sums)
            totals = add_group(vx, sums, totals)
        put_sums(sums_ref, y, totals)

    advance(0, True)
    advance(1, True)

    def body(step, carry):
        advance(step, False)
        return carry

    lax.fori_loop(2, Y, body, 0)
    send(sz, vert_index, out, sums_ref, mirror, packet, right, left)


def last_kernel(sz, *refs):
    state, inner, mirror_in, right_in, left_in, packet_in, wall, xw, yw, emission = refs[:10]
    others = refs[10 : 10 + sz.vert - 2]
    result, spread, along, turn_a, turn_b, final, sems = refs[10 + sz.vert - 2 :]
    parity = lax.axis_index("vert") % 2
    received(sz, parity, mirror_in, packet_in, others, spread)
    flux = spread[FIELDS - 1, block(real_row(parity, 0) * SUB), :]
    beyond = wall_part(sz, mirror_in, wall, emission, flux, yw)

    def prepare(step, carry):
        _, uy, inv_t, amount, _, py, _, _ = field_rows(spread, real_row(parity, step))
        for kg in range(sz.kg):
            for r, value in enumerate(part_y(sz, yw, kg, uy, inv_t, amount, py)):
                along[3 * kg + r, block(step * SUB), :] = value
        return carry

    lax.fori_loop(0, Y, prepare, 0)
    for xg in range(sz.xg):
        turn = turn_b if xg % 2 else turn_a
        vx = xw[4 * xg]
        for step in range(Y):
            y = real_row(parity, step)
            rows = pl.ds(step * SUB, SUB)
            ux, _, inv_t, _, px, _, half_theta, rate = field_rows(spread, y)
            along_x = part_x(vx, ux, inv_t, px)
            for kg in range(sz.kg):
                t = xg * sz.kg + kg
                along_y = [along[3 * kg + r, rows, :] for r in range(3)]
                for f, source in enumerate(target(along_x, along_y, half_theta)):
                    at = pl.ds(sz.base(f, t) + step * SUB, SUB)
                    edge = side_edge(sz, right_in, left_in, f, t, step)
                    moved = (inner[at, :] + edge) + (source - rate * state[at, :])
                    if step < 2:
                        moved = moved + beyond(step, f, t)
                    turn[2 * kg + f, block(y * SUB), :] = moved
        for f in range(2):
            for kg in range(sz.kg):
                parts = []
                for x in range(SUB):
                    for part in range(0, Y, SUB):
                        parts.append(turn[2 * kg + f, pl.ds(part * SUB + x, SUB, stride=SUB), :])
                turned = jnp.concatenate(parts, axis=0).T
                for k in range(kg * PART_K, min((kg + 1) * PART_K, sz.band)):
                    row = (k - kg * PART_K) * PART_X
                    final[f, k, xg * PART_X : (xg + 1) * PART_X, :] = turned[row : row + PART_X, :]
            group_copy(sz, final, result, sems, f, xg).start()
    for xg in range(sz.xg):
        for f in range(2):
            group_copy(sz, final, result, sems, f, xg).wait()


def shapes(sz):
    f32 = jnp.float32
    side = jax.ShapeDtypeStruct((sz.side_rows, LANES), f32)
    return (
        jax.ShapeDtypeStruct((sz.state_rows, LANES), f32),
        jax.ShapeDtypeStruct((sz.mirror_blocks + 2, SUB, LANES), f32),
        jax.ShapeDtypeStruct((ROWS, sz.cells), f32),
        side,
        side,
    )


def on_device(distribution, wall_type, wall_temp_index, wall_temps, accommodation):
    _, band, nx, cells = distribution.shape
    vert = lax.axis_size("vert")
    columns = lax.axis_size("gx")
    sz = Sizes(band, nx, cells, vert)
    vmem = pl.BlockSpec(memory_space=pltpu.VMEM)
    smem = pl.BlockSpec(memory_space=pltpu.SMEM)
    hbm = pl.BlockSpec(memory_space=pltpu.HBM)
    final_shape = jax.ShapeDtypeStruct(distribution.shape, jnp.float32)
    bytes_moved = 2 * distribution.size * 4
    sums_scratch = pltpu.VMEM((FIELDS, sz.cells, LANES), jnp.float32)
    turn_scratch = [pltpu.VMEM((2 * sz.kg, sz.cells, LANES), jnp.float32)] * 2
    step_scratch = [pltpu.VMEM((FIELDS, sz.cells, LANES), jnp.float32)]
    first_vmem = ALL_VMEM - 26 * distribution.size
    stage = [
        pltpu.VMEM(distribution.shape, jnp.float32),
        pltpu.SemaphoreType.DMA((2 * sz.xg,)),
    ]
    state, mirror, packet, right, left = pl.pallas_call(
        functools.partial(first_kernel, sz),
        out_shape=shapes(sz),
        in_specs=[hbm],
        out_specs=(vmem,) * 5,
        scratch_shapes=[sums_scratch] + turn_scratch + stage,
        cost_estimate=pl.CostEstimate(
            flops=10 * distribution.size, bytes_accessed=bytes_moved, transcendentals=0
        ),
        compiler_params=pltpu.CompilerParams(vmem_limit_bytes=first_vmem),
        name="first",
    )(distribution)
    tables = pl.pallas_call(
        functools.partial(wall_kernel, sz),
        out_shape=tuple(
            jax.ShapeDtypeStruct((count, SUB, LANES), jnp.float32)
            for count in (1, 4 * sz.xg, 4 * sz.kg, 2 * sz.tiles)
        ),
        in_specs=[smem] * 4,
        out_specs=(vmem,) * 4,
        compiler_params=pltpu.CompilerParams(vmem_limit_bytes=KERNEL_VMEM),
        name="walls",
    )(wall_type, wall_temp_index, wall_temps, accommodation)
    ring = [(i, (i + 1) % columns) for i in range(columns)]
    back = [(j, i) for i, j in ring]
    for iteration in range(ITERS):
        last = iteration == ITERS - 1
        mirror_in = lax.ppermute(mirror, "vert", [(s, s ^ 1) for s in range(vert)])
        right_in = lax.ppermute(right, "gx", ring)
        left_in = lax.ppermute(left, "gx", back)
        others = []
        for mask in range(vert - 1, 1, -1):
            others.append(lax.ppermute(packet, "vert", [(s, s ^ mask) for s in range(vert)]))
        inner = pl.pallas_call(
            functools.partial(advect_kernel, sz),
            out_shape=jax.ShapeDtypeStruct((sz.state_rows, LANES), jnp.float32),
            in_specs=[vmem] * 3,
            out_specs=vmem,
            cost_estimate=pl.CostEstimate(
                flops=12 * distribution.size, bytes_accessed=bytes_moved, transcendentals=0
            ),
            compiler_params=pltpu.CompilerParams(vmem_limit_bytes=KERNEL_VMEM),
            name="advect",
        )(state, tables[1], tables[2])
        if last:
            along = pltpu.VMEM((3 * sz.kg, sz.cells, LANES), jnp.float32)
            scratch = step_scratch + [along] + turn_scratch + stage
        else:
            scratch = step_scratch + [sums_scratch]
        result = pl.pallas_call(
            functools.partial(last_kernel if last else step_kernel, sz),
            out_shape=(final_shape,) if last else shapes(sz),
            in_specs=[vmem] * (10 + len(others)),
            out_specs=(hbm,) if last else (vmem,) * 5,
            scratch_shapes=scratch,
            cost_estimate=pl.CostEstimate(
                flops=40 * distribution.size, bytes_accessed=bytes_moved, transcendentals=0
            ),
            compiler_params=pltpu.CompilerParams(vmem_limit_bytes=KERNEL_VMEM),
            name="last" if last else "step",
        )(state, inner, mirror_in, right_in, left_in, packet, *tables, *others)
        if last:
            (state,) = result
        else:
            state, mirror, packet, right, left = result
    return state


def solution(mesh):
    placed = (P(None, "vert", None, "gx"), P(None, "gx"), P(None, "gx"), P(), P())
    return jax.shard_map(
        on_device,
        mesh=mesh,
        in_specs=placed,
        out_specs=P(None, "vert", None, "gx"),
        check_vma=False,
    )
```

```python
import functools
import math

import jax
import jax.numpy as jnp
from jax import lax
from jax.experimental import pallas as pl
from jax.experimental.pallas import tpu as pltpu
from jax.sharding import PartitionSpec as P


Y = 16
ITERS = 4
NTEMP = 2
NTYPE = 3
SUB = 8
LANES = 128
ROWS = 16
PART_X = 16
PART_K = LANES // PART_X
FIELDS = 9
KERNEL_VMEM = 16 * 1024 * 1024
ALL_VMEM = 64 * 1024 * 1024

vmax_speed = 4.5
courant = 0.5
diffusivity_ratio = 2.0 / 3.0
relaxation_multiplier = 2.5
shear_exponent = 0.19
time_increment = courant / vmax_speed


class Sizes:
    def __init__(self, band, nx, cells, vert):
        assert cells == SUB * Y and nx % (2 * PART_X) == 0
        self.band, self.nx, self.cells, self.vert = band, nx, cells, vert
        self.nv = band * vert
        self.xg = nx // PART_X
        self.kg = -(-band // PART_K)
        self.tiles = self.xg * self.kg
        self.half = self.tiles // 2
        self.state_rows = 2 * self.tiles * cells
        self.side_rows = 2 * self.half * Y * 2 + 2 * SUB
        self.mirror_blocks = 4 * self.tiles
        self.weight = 2.0 * vmax_speed / nx * (2.0 * vmax_speed / self.nv)

    def base(self, f, t):
        return (f * self.tiles + t) * self.cells

    def side_base(self, f, t):
        return SUB + (f * self.half + t % self.half) * 2 * Y

    def mirror_index(self, d, f, t):
        return (d * 2 + f) * self.tiles + t


def node_speed(index, number):
    return vmax_speed * (2.0 * index.astype(jnp.float32) + 1.0 - number) / number


def row_speed(sz, vert_index, offset):
    lower = vert_index // 2 * sz.band + offset
    return node_speed(jnp.where(vert_index % 2 == 0, lower, sz.nv - 1 - lower), sz.nv)


def beam_weights(speed):
    s = jnp.abs(speed) * time_increment
    return -1.5 * s + 0.5 * s * s, 2.0 * s - s * s, -0.5 * s + 0.5 * s * s


def lane():
    return lax.broadcasted_iota(jnp.int32, (SUB, LANES), 1)


def sub():
    return lax.broadcasted_iota(jnp.int32, (SUB, LANES), 0)


def x_speed(sz, group):
    return node_speed(group * PART_X + lane() % PART_X, sz.nx)


def y_speed(sz, vert_index, group):
    return row_speed(sz, vert_index, group * PART_K + lane() // PART_X)


def inside(sz, group):
    if (group + 1) * PART_K <= sz.band:
        return None
    return group * PART_K + lane() // PART_X < sz.band


def masked(mask, value):
    return value if mask is None else jnp.where(mask, value, 0.0)


def real_row(parity, step):
    return jnp.where(parity == 0, Y - 1 - step, step)


def block(start):
    return pl.ds(pl.multiple_of(start, SUB), SUB)


def add_columns(vy, g, h, sums):
    p = vy * g
    q = vy * p
    r = vy * (q + h)
    new = (g, p, q, r, h)
    return new if sums is None else tuple(a + b for a, b in zip(sums, new))


def add_group(vx, sums, totals):
    t0, t1, t2, t3, u0 = sums
    a = vx * t0
    b = vx * a
    c = vx * t1
    new = (t0, a, t1, b, c, t2, u0, vx * (b + t2 + u0), vx * c + t3)
    return new if totals is None else tuple(x + y for x, y in zip(totals, new))


def put_sums(sums_ref, y, totals):
    for m, total in enumerate(totals):
        sums_ref[m, block(y * SUB), :] = total


def send(sz, vert_index, state, sums_ref, mirror, packet, right, left):
    rows = []
    for m in range(FIELDS):
        rows.append(jnp.sum(sums_ref[m].T, axis=0, keepdims=True) * sz.weight)
    n, mx, my, pxx, pxy, pyy, extra, tx, ty = rows
    even = vert_index % 2 == 0
    zero = jnp.zeros_like(n)
    rows = [n, mx, my, pxx + pyy + extra, pxx, pxy, pyy, tx, ty]
    rows += [jnp.where(even, -my, zero), jnp.where(even, zero, my)]
    rows += [zero] * (ROWS - len(rows))
    for r, value in enumerate(rows):
        packet[r : r + 1, :] = value
        mirror[sz.mirror_blocks + r // SUB, r % SUB : r % SUB + 1, :] = value
    for f in range(2):
        for t in range(sz.tiles):
            base = sz.base(f, t)
            for d in range(2):
                mirror[sz.mirror_index(d, f, t)] = state[pl.ds(base + (Y - 1 - d) * SUB, SUB), :]
            positive = t >= sz.half
            out = right if positive else left
            side = sz.side_base(f, t)
            _, x1, x2 = beam_weights(x_speed(sz, t // sz.kg))
            ends = (SUB - 1, SUB - 2) if positive else (0, 1)
            for part in range(0, Y, SUB):
                near, far = [
                    state[pl.ds(base + part * SUB + c, SUB, stride=SUB), :] for c in ends
                ]
                pair = (x1 * near + x2 * far, x2 * near)
                for c in range(2):
                    value = pair[c] if positive else pair[1 - c]
                    out[pl.ds(side + 2 * part + c, SUB, stride=2), :] = value
    pad = jnp.zeros((SUB, LANES), jnp.float32)
    for out in (right, left):
        out[0:SUB, :] = pad
        out[sz.side_rows - SUB : sz.side_rows, :] = pad


def wall_kernel(sz, type_ref, index_ref, temps_ref, acc_ref, wall, xw, yw, emission):
    face = 1 - lax.axis_index("vert") % 2
    column = sub()
    kind = jnp.zeros_like(column)
    entry = jnp.zeros_like(column)
    for x in range(SUB):
        kind = jnp.where(column == x, type_ref[face, x], kind)
        entry = jnp.where(column == x, index_ref[face, x], entry)
    percent = jnp.zeros_like(column)
    for t in range(NTYPE):
        percent = jnp.where(kind == t, acc_ref[t], percent)
    alpha = percent.astype(jnp.float32) / 100.0
    heat = jnp.ones((SUB, LANES), jnp.float32)
    denom = jnp.ones((SUB, LANES), jnp.float32)

    def grid(number):
        index = lax.broadcasted_iota(jnp.int32, (1, -(-number // LANES) * LANES), 1)
        return node_speed(index, number), index < number

    vx, in_x = grid(sz.nx)
    vy, in_y = grid(sz.nv)
    for t in range(NTEMP):
        temp = jnp.full((1, 1), temps_ref[t], jnp.float32)
        along = jnp.sum(jnp.where(in_x, jnp.exp(-vx * vx / temp), 0.0), axis=1, keepdims=True)
        across = jnp.sum(
            jnp.where(in_y, jnp.maximum(vy, 0.0) * jnp.exp(-vy * vy / temp), 0.0),
            axis=1,
            keepdims=True,
        )
        inward = sz.weight * along * across / (math.pi * temp)
        heat = jnp.where(entry == t, temp, heat)
        denom = jnp.where(entry == t, inward, denom)
    wall[0] = 1.0 - alpha
    emitted = alpha / (denom * (math.pi * heat))
    vert_index = lax.axis_index("vert")
    inv_heat = 1.0 / heat
    wall_y = []
    for kg in range(sz.kg):
        vy = y_speed(sz, vert_index, kg)
        for r, value in enumerate((vy,) + beam_weights(vy)):
            yw[4 * kg + r] = value
        wall_y.append(masked(inside(sz, kg), emitted * jnp.exp(-vy * vy * inv_heat)))
    for xg in range(sz.xg):
        vx = x_speed(sz, xg)
        for r, value in enumerate((vx,) + beam_weights(vx)):
            xw[4 * xg + r] = value
        wall_x = jnp.exp(-vx * vx * inv_heat)
        for kg in range(sz.kg):
            diffuse = wall_x * wall_y[kg]
            emission[xg * sz.kg + kg] = diffuse
            emission[sz.tiles + xg * sz.kg + kg] = 0.5 * heat * diffuse


def group_copy(sz, source, target, sems, f, xg):
    speeds = pl.ds(xg * PART_X, PART_X)
    return pltpu.make_async_copy(
        source.at[f, :, speeds], target.at[f, :, speeds], sems.at[f * sz.xg + xg]
    )


def chunk_copy(sz, source, target, sems, f, kg):
    rows = pl.ds(kg * PART_K, min(PART_K, sz.band - kg * PART_K))
    return pltpu.make_async_copy(
        source.at[f, rows], target.at[f, rows], sems.at[f * sz.kg + kg]
    )


def first_kernel(sz, argument, state, mirror, packet, right, left, sums_ref, turn_a, turn_b, given, sems):
    vert_index = lax.axis_index("vert")
    parity = vert_index % 2
    for xg in range(sz.xg):
        for f in range(2):
            group_copy(sz, argument, given, sems, f, xg).start()
    for xg in range(sz.xg):
        turn = turn_b if xg % 2 else turn_a
        if xg % (sz.xg // 2) == 0:
            for other in range(xg, xg + sz.xg // 2):
                for f in range(2):
                    group_copy(sz, argument, given, sems, f, other).wait()
        for kg in range(sz.kg):
            for f in range(2):
                parts = []
                for k in range(kg * PART_K, (kg + 1) * PART_K):
                    if k < sz.band:
                        parts.append(given[f, k, xg * PART_X : (xg + 1) * PART_X, :])
                    else:
                        parts.append(jnp.zeros((PART_X, sz.cells), jnp.float32))
                turned = jnp.concatenate(parts, axis=0).T
                slot = 2 * kg + f
                for x in range(SUB):
                    for part in range(0, Y, SUB):
                        piece = turned[x * Y + part : x * Y + part + SUB, :]
                        turn[slot, pl.ds(part * SUB + x, SUB, stride=SUB), :] = piece
        vx = x_speed(sz, xg)
        for step in range(Y):
            y = real_row(parity, step)
            sums = None
            for kg in range(sz.kg):
                g, h = [turn[2 * kg + f, block(y * SUB), :] for f in range(2)]
                for f, value in enumerate((g, h)):
                    state[pl.ds(sz.base(f, xg * sz.kg + kg) + step * SUB, SUB), :] = value
                sums = add_columns(y_speed(sz, vert_index, kg), g, h, sums)
            for m, total in enumerate(add_group(vx, sums, None)):
                if xg:
                    total = total + sums_ref[m, block(y * SUB), :]
                sums_ref[m, block(y * SUB), :] = total
    send(sz, vert_index, state, sums_ref, mirror, packet, right, left)


def fields_of(parity, tot):
    def row(r):
        return tot[r // SUB][r % SUB : r % SUB + 1, :]

    n, mx, my, energy, pxx, pxy, pyy, tx, ty = [row(r) for r in range(9)]
    inv_n = 1.0 / n
    ux, uy = mx * inv_n, my * inv_n
    usq = ux * ux + uy * uy
    theta = 2.0 / 3.0 * (energy * inv_n - usq)
    along = ux * mx + uy * my
    qx = tx - 2.0 * (ux * pxx + uy * pxy) + usq * mx - ux * energy + 2.0 * ux * along - ux * usq * n
    qy = ty - 2.0 * (ux * pxy + uy * pyy) + usq * my - uy * energy + 2.0 * uy * along - uy * usq * n
    inv_t = 1.0 / theta
    rate = (time_increment * relaxation_multiplier) * n * jnp.exp(shear_exponent * jnp.log(theta))
    amount = rate * n * inv_t * (1.0 / math.pi)
    scale = (1.0 - diffusivity_ratio) * 0.8 * inv_n * inv_t * inv_t
    flux = jnp.where(parity == 0, row(10), row(9))
    return [ux, uy, inv_t, amount, scale * qx, scale * qy, 0.5 * theta, rate, flux]


def advect_kernel(sz, state, xw, yw, out):
    column = sub()

    def advance(step, near_at, far_at):
        for xg in range(sz.xg):
            x0 = 1.0 + xw[4 * xg + 1]
            x1, x2 = xw[4 * xg + 2], xw[4 * xg + 3]
            for kg in range(sz.kg):
                t = xg * sz.kg + kg
                c0 = x0 + yw[4 * kg + 1]
                y1, y2 = yw[4 * kg + 2], yw[4 * kg + 3]
                for f in range(2):
                    at = sz.base(f, t) + step * SUB
                    v = state[block(at), :]
                    if t >= sz.half:
                        one = jnp.where(column < 1, 0.0, state[pl.ds(at - 1, SUB), :])
                        two = jnp.where(column < 2, 0.0, state[pl.ds(at - 2, SUB), :])
                    else:
                        one = jnp.where(column >= SUB - 1, 0.0, state[pl.ds(at + 1, SUB), :])
                        two = jnp.where(column >= SUB - 2, 0.0, state[pl.ds(at + 2, SUB), :])
                    moved = v * c0 + (x1 * one + x2 * two)
                    if near_at:
                        moved = moved + y1 * state[block(at - SUB), :]
                    if far_at:
                        moved = moved + y2 * state[block(at - 2 * SUB), :]
                    out[block(at), :] = moved

    advance(0, False, False)
    advance(1, True, False)

    def body(step, carry):
        advance(step, True, True)
        return carry

    lax.fori_loop(2, Y, body, 0)


def spread_fields(sz, rows, spread):
    index = lax.broadcasted_iota(jnp.int32, (ROWS, LANES), 0)
    table = jnp.zeros((ROWS, sz.cells), jnp.float32)
    for r, value in enumerate(rows):
        table = jnp.where(index == r, value, table)
    parts = []
    for _ in range(3):
        part = table.astype(jnp.bfloat16)
        parts.append(part)
        table = table - part.astype(jnp.float32)
    parts = jnp.concatenate(parts, axis=0)
    index = lax.broadcasted_iota(jnp.int32, (3 * ROWS, LANES), 0) % ROWS
    picks = [(index == r).astype(jnp.float32).astype(jnp.bfloat16) for r in range(FIELDS)]
    wide = lax.dot_general(
        parts, jnp.concatenate(picks, axis=1), (((0,), (0,)), ((), ())),
        preferred_element_type=jnp.float32,
    )
    for r in range(FIELDS):
        spread[r] = wide[:, r * LANES : (r + 1) * LANES]


def received(sz, parity, mirror_in, packet_in, others, spread):
    tot = [packet_in[SUB * b : SUB * b + SUB, :] + mirror_in[sz.mirror_blocks + b] for b in range(2)]
    for other in others:
        tot = [tot[b] + other[SUB * b : SUB * b + SUB, :] for b in range(2)]
    spread_fields(sz, fields_of(parity, tot), spread)


def side_edge(sz, right_in, left_in, f, t, step):
    column = sub()
    side = sz.side_base(f, t) + 2 * step
    if t >= sz.half:
        return jnp.where(column < 2, right_in[pl.ds(side, SUB), :], 0.0)
    start = side - (SUB - 2)
    return jnp.where(column >= SUB - 2, left_in[pl.ds(start, SUB), :], 0.0)


def field_rows(spread, y):
    return [spread[r, block(y * SUB), :] for r in range(FIELDS - 1)]


def part_y(sz, yw, kg, uy, inv_t, amount, py):
    cy = yw[4 * kg] - uy
    cy_sq = cy * cy * inv_t
    return masked(inside(sz, kg), amount * jnp.exp(-cy_sq)), py * cy, cy_sq - 2.0


def part_x(vx, ux, inv_t, px):
    cx = vx - ux
    cx_sq = cx * cx * inv_t
    return jnp.exp(-cx_sq), px * cx, cx_sq


def target(along_x, along_y, half_theta):
    ex, pxs, cx_sq = along_x
    ey, pys, cys = along_y
    maxwell = ex * ey
    p = pxs + pys
    sg = maxwell * (1.0 + p * (cx_sq + cys))
    return sg, half_theta * (sg + p * maxwell)


def wall_part(sz, mirror_in, wall, emission, flux, yw):
    def ghost(d, f, t):
        return wall[0] * mirror_in[sz.mirror_index(d, f, t)] + flux * emission[f * sz.tiles + t]

    def beyond(step, f, t):
        kg = t % sz.kg
        y1, y2 = yw[4 * kg + 2], yw[4 * kg + 3]
        if step == 0:
            return y1 * ghost(0, f, t) + y2 * ghost(1, f, t)
        return y2 * ghost(0, f, t)

    return beyond


def step_kernel(sz, *refs):
    state, inner, mirror_in, right_in, left_in, packet_in, wall, xw, yw, emission = refs[:10]
    others = refs[10 : 10 + sz.vert - 2]
    out, mirror, packet, right, left, spread, sums_ref = refs[10 + sz.vert - 2 :]
    vert_index = lax.axis_index("vert")
    parity = vert_index % 2
    received(sz, parity, mirror_in, packet_in, others, spread)
    flux = spread[FIELDS - 1, block(real_row(parity, 0) * SUB), :]
    beyond = wall_part(sz, mirror_in, wall, emission, flux, yw)

    def advance(step, near_wall):
        y = real_row(parity, step)
        ux, uy, inv_t, amount, px, py, half_theta, rate = field_rows(spread, y)
        along_y = [part_y(sz, yw, kg, uy, inv_t, amount, py) for kg in range(sz.kg)]
        totals = None
        for xg in range(sz.xg):
            vx = xw[4 * xg]
            along_x = part_x(vx, ux, inv_t, px)
            sums = None
            for kg in range(sz.kg):
                t = xg * sz.kg + kg
                values = []
                for f, source in enumerate(target(along_x, along_y[kg], half_theta)):
                    at = sz.base(f, t) + step * SUB
                    edge = side_edge(sz, right_in, left_in, f, t, step)
                    moved = (inner[block(at), :] + edge) + (source - rate * state[block(at), :])
                    if near_wall:
                        moved = moved + beyond(step, f, t)
                    out[block(at), :] = moved
                    values.append(moved)
                sums = add_columns(yw[4 * kg], values[0], values[1], sums)
            totals = add_group(vx, sums, totals)
        put_sums(sums_ref, y, totals)

    advance(0, True)
    advance(1, True)

    def body(step, carry):
        advance(step, False)
        return carry

    lax.fori_loop(2, Y, body, 0)
    send(sz, vert_index, out, sums_ref, mirror, packet, right, left)


def last_kernel(sz, *refs):
    state, inner, mirror_in, right_in, left_in, packet_in, wall, xw, yw, emission = refs[:10]
    others = refs[10 : 10 + sz.vert - 2]
    result, spread, along, turn_a, turn_b, final, sems = refs[10 + sz.vert - 2 :]
    parity = lax.axis_index("vert") % 2
    received(sz, parity, mirror_in, packet_in, others, spread)
    flux = spread[FIELDS - 1, block(real_row(parity, 0) * SUB), :]
    beyond = wall_part(sz, mirror_in, wall, emission, flux, yw)

    def prepare(step, carry):
        rows = block(step * SUB)
        ux, uy, inv_t, amount, px, py, _, _ = field_rows(spread, real_row(parity, step))
        for kg in range(sz.kg):
            for r, value in enumerate(part_y(sz, yw, kg, uy, inv_t, amount, py)):
                along[3 * kg + r, rows, :] = value
        for xg in range(sz.xg):
            for r, value in enumerate(part_x(xw[4 * xg], ux, inv_t, px)):
                along[3 * (sz.kg + xg) + r, rows, :] = value
        return carry

    lax.fori_loop(0, Y, prepare, 0)
    for kg in range(sz.kg):
        for xg in range(sz.xg):
            turn = turn_b if xg % 2 else turn_a
            t = xg * sz.kg + kg
            for step in range(Y):
                y = real_row(parity, step)
                rows = pl.ds(step * SUB, SUB)
                half_theta, rate = [spread[r, block(y * SUB), :] for r in (6, 7)]
                along_y = [along[3 * kg + r, rows, :] for r in range(3)]
                along_x = [along[3 * (sz.kg + xg) + r, rows, :] for r in range(3)]
                for f, source in enumerate(target(along_x, along_y, half_theta)):
                    at = pl.ds(sz.base(f, t) + step * SUB, SUB)
                    edge = side_edge(sz, right_in, left_in, f, t, step)
                    moved = (inner[at, :] + edge) + (source - rate * state[at, :])
                    if step < 2:
                        moved = moved + beyond(step, f, t)
                    turn[f, block(y * SUB), :] = moved
            for f in range(2):
                parts = []
                for x in range(SUB):
                    for part in range(0, Y, SUB):
                        parts.append(turn[f, pl.ds(part * SUB + x, SUB, stride=SUB), :])
                turned = jnp.concatenate(parts, axis=0).T
                for k in range(kg * PART_K, min((kg + 1) * PART_K, sz.band)):
                    row = (k - kg * PART_K) * PART_X
                    final[f, k, xg * PART_X : (xg + 1) * PART_X, :] = turned[row : row + PART_X, :]
        for f in range(2):
            chunk_copy(sz, final, result, sems, f, kg).start()
    for kg in range(sz.kg):
        for f in range(2):
            chunk_copy(sz, final, result, sems, f, kg).wait()


def shapes(sz):
    f32 = jnp.float32
    side = jax.ShapeDtypeStruct((sz.side_rows, LANES), f32)
    return (
        jax.ShapeDtypeStruct((sz.state_rows, LANES), f32),
        jax.ShapeDtypeStruct((sz.mirror_blocks + 2, SUB, LANES), f32),
        jax.ShapeDtypeStruct((ROWS, sz.cells), f32),
        side,
        side,
    )


def on_device(distribution, wall_type, wall_temp_index, wall_temps, accommodation):
    _, band, nx, cells = distribution.shape
    vert = lax.axis_size("vert")
    columns = lax.axis_size("gx")
    sz = Sizes(band, nx, cells, vert)
    vmem = pl.BlockSpec(memory_space=pltpu.VMEM)
    smem = pl.BlockSpec(memory_space=pltpu.SMEM)
    hbm = pl.BlockSpec(memory_space=pltpu.HBM)
    final_shape = jax.ShapeDtypeStruct(distribution.shape, jnp.float32)
    bytes_moved = 2 * distribution.size * 4
    sums_scratch = pltpu.VMEM((FIELDS, sz.cells, LANES), jnp.float32)
    turn_scratch = [pltpu.VMEM((2 * sz.kg, sz.cells, LANES), jnp.float32)] * 2
    step_scratch = [pltpu.VMEM((FIELDS, sz.cells, LANES), jnp.float32)]
    first_vmem = ALL_VMEM - 26 * distribution.size
    stage = [
        pltpu.VMEM(distribution.shape, jnp.float32),
        pltpu.SemaphoreType.DMA((2 * max(sz.xg, sz.kg),)),
    ]
    state, mirror, packet, right, left = pl.pallas_call(
        functools.partial(first_kernel, sz),
        out_shape=shapes(sz),
        in_specs=[hbm],
        out_specs=(vmem,) * 5,
        scratch_shapes=[sums_scratch] + turn_scratch + stage,
        cost_estimate=pl.CostEstimate(
            flops=10 * distribution.size, bytes_accessed=bytes_moved, transcendentals=0
        ),
        compiler_params=pltpu.CompilerParams(vmem_limit_bytes=first_vmem),
        name="first",
    )(distribution)
    tables = pl.pallas_call(
        functools.partial(wall_kernel, sz),
        out_shape=tuple(
            jax.ShapeDtypeStruct((count, SUB, LANES), jnp.float32)
            for count in (1, 4 * sz.xg, 4 * sz.kg, 2 * sz.tiles)
        ),
        in_specs=[smem] * 4,
        out_specs=(vmem,) * 4,
        compiler_params=pltpu.CompilerParams(vmem_limit_bytes=KERNEL_VMEM),
        name="walls",
    )(wall_type, wall_temp_index, wall_temps, accommodation)
    ring = [(i, (i + 1) % columns) for i in range(columns)]
    back = [(j, i) for i, j in ring]
    for iteration in range(ITERS):
        last = iteration == ITERS - 1
        mirror_in = lax.ppermute(mirror, "vert", [(s, s ^ 1) for s in range(vert)])
        right_in = lax.ppermute(right, "gx", ring)
        left_in = lax.ppermute(left, "gx", back)
        others = []
        for mask in range(vert - 1, 1, -1):
            others.append(lax.ppermute(packet, "vert", [(s, s ^ mask) for s in range(vert)]))
        inner = pl.pallas_call(
            functools.partial(advect_kernel, sz),
            out_shape=jax.ShapeDtypeStruct((sz.state_rows, LANES), jnp.float32),
            in_specs=[vmem] * 3,
            out_specs=vmem,
            cost_estimate=pl.CostEstimate(
                flops=12 * distribution.size, bytes_accessed=bytes_moved, transcendentals=0
            ),
            compiler_params=pltpu.CompilerParams(vmem_limit_bytes=KERNEL_VMEM),
            name="advect",
        )(state, tables[1], tables[2])
        if last:
            along = pltpu.VMEM((3 * (sz.kg + sz.xg), sz.cells, LANES), jnp.float32)
            scratch = step_scratch + [along] + turn_scratch + stage
        else:
            scratch = step_scratch + [sums_scratch]
        result = pl.pallas_call(
            functools.partial(last_kernel if last else step_kernel, sz),
            out_shape=(final_shape,) if last else shapes(sz),
            in_specs=[vmem] * (10 + len(others)),
            out_specs=(hbm,) if last else (vmem,) * 5,
            scratch_shapes=scratch,
            cost_estimate=pl.CostEstimate(
                flops=40 * distribution.size, bytes_accessed=bytes_moved, transcendentals=0
            ),
            compiler_params=pltpu.CompilerParams(vmem_limit_bytes=KERNEL_VMEM),
            name="last" if last else "step",
        )(state, inner, mirror_in, right_in, left_in, packet, *tables, *others)
        if last:
            (state,) = result
        else:
            state, mirror, packet, right, left = result
    return state


def solution(mesh):
    placed = (P(None, "vert", None, "gx"), P(None, "gx"), P(None, "gx"), P(), P())
    return jax.shard_map(
        on_device,
        mesh=mesh,
        in_specs=placed,
        out_specs=P(None, "vert", None, "gx"),
        check_vma=False,
    )
```

```python
import functools
import math

import jax
import jax.numpy as jnp
from jax import lax
from jax.experimental import pallas as pl
from jax.experimental.pallas import tpu as pltpu
from jax.sharding import PartitionSpec as P


Y = 16
ITERS = 4
NTEMP = 2
NTYPE = 3
SUB = 8
LANES = 128
ROWS = 16
PART_X = 16
PART_K = LANES // PART_X
FIELDS = 9
KERNEL_VMEM = 16 * 1024 * 1024
ALL_VMEM = 64 * 1024 * 1024

vmax_speed = 4.5
courant = 0.5
diffusivity_ratio = 2.0 / 3.0
relaxation_multiplier = 2.5
shear_exponent = 0.19
time_increment = courant / vmax_speed


class Sizes:
    def __init__(self, band, nx, cells, vert):
        assert cells == SUB * Y and nx % (2 * PART_X) == 0
        self.band, self.nx, self.cells, self.vert = band, nx, cells, vert
        self.nv = band * vert
        self.xg = nx // PART_X
        self.kg = -(-band // PART_K)
        self.tiles = self.xg * self.kg
        self.half = self.tiles // 2
        self.state_rows = 2 * self.tiles * cells
        self.side_rows = 2 * self.half * Y * 2 + 2 * SUB
        self.mirror_blocks = 4 * self.tiles
        self.weight = 2.0 * vmax_speed / nx * (2.0 * vmax_speed / self.nv)

    def base(self, f, t):
        return (f * self.tiles + t) * self.cells

    def side_base(self, f, t):
        return SUB + (f * self.half + t % self.half) * 2 * Y

    def mirror_index(self, d, f, t):
        return (d * 2 + f) * self.tiles + t


def node_speed(index, number):
    return vmax_speed * (2.0 * index.astype(jnp.float32) + 1.0 - number) / number


def row_speed(sz, vert_index, offset):
    lower = vert_index // 2 * sz.band + offset
    return node_speed(jnp.where(vert_index % 2 == 0, lower, sz.nv - 1 - lower), sz.nv)


def beam_weights(speed):
    s = jnp.abs(speed) * time_increment
    return -1.5 * s + 0.5 * s * s, 2.0 * s - s * s, -0.5 * s + 0.5 * s * s


def lane():
    return lax.broadcasted_iota(jnp.int32, (SUB, LANES), 1)


def sub():
    return lax.broadcasted_iota(jnp.int32, (SUB, LANES), 0)


def x_speed(sz, group):
    return node_speed(group * PART_X + lane() % PART_X, sz.nx)


def y_speed(sz, vert_index, group):
    return row_speed(sz, vert_index, group * PART_K + lane() // PART_X)


def inside(sz, group):
    if (group + 1) * PART_K <= sz.band:
        return None
    return group * PART_K + lane() // PART_X < sz.band


def masked(mask, value):
    return value if mask is None else jnp.where(mask, value, 0.0)


def real_row(parity, step):
    return jnp.where(parity == 0, Y - 1 - step, step)


def block(start):
    return pl.ds(pl.multiple_of(start, SUB), SUB)


def add_columns(vy, g, h, sums):
    p = vy * g
    q = vy * p
    r = vy * (q + h)
    new = (g, p, q, r, h)
    return new if sums is None else tuple(a + b for a, b in zip(sums, new))


def add_group(vx, sums, totals):
    t0, t1, t2, t3, u0 = sums
    a = vx * t0
    b = vx * a
    c = vx * t1
    new = (t0, a, t1, b, c, t2, u0, vx * (b + t2 + u0), vx * c + t3)
    return new if totals is None else tuple(x + y for x, y in zip(totals, new))


def put_sums(sums_ref, y, totals):
    for m, total in enumerate(totals):
        sums_ref[m, block(y * SUB), :] = total


def send(sz, vert_index, state, sums_ref, mirror, packet, right, left):
    rows = []
    for m in range(FIELDS):
        rows.append(jnp.sum(sums_ref[m].T, axis=0, keepdims=True) * sz.weight)
    n, mx, my, pxx, pxy, pyy, extra, tx, ty = rows
    even = vert_index % 2 == 0
    zero = jnp.zeros_like(n)
    rows = [n, mx, my, pxx + pyy + extra, pxx, pxy, pyy, tx, ty]
    rows += [jnp.where(even, -my, zero), jnp.where(even, zero, my)]
    rows += [zero] * (ROWS - len(rows))
    for r, value in enumerate(rows):
        packet[r : r + 1, :] = value
        mirror[sz.mirror_blocks + r // SUB, r % SUB : r % SUB + 1, :] = value
    for f in range(2):
        for t in range(sz.tiles):
            base = sz.base(f, t)
            for d in range(2):
                mirror[sz.mirror_index(d, f, t)] = state[pl.ds(base + (Y - 1 - d) * SUB, SUB), :]
            positive = t >= sz.half
            out = right if positive else left
            side = sz.side_base(f, t)
            _, x1, x2 = beam_weights(x_speed(sz, t // sz.kg))
            ends = (SUB - 1, SUB - 2) if positive else (0, 1)
            for part in range(0, Y, SUB):
                near, far = [
                    state[pl.ds(base + part * SUB + c, SUB, stride=SUB), :] for c in ends
                ]
                pair = (x1 * near + x2 * far, x2 * near)
                for c in range(2):
                    value = pair[c] if positive else pair[1 - c]
                    out[pl.ds(side + 2 * part + c, SUB, stride=2), :] = value
    pad = jnp.zeros((SUB, LANES), jnp.float32)
    for out in (right, left):
        out[0:SUB, :] = pad
        out[sz.side_rows - SUB : sz.side_rows, :] = pad


def wall_kernel(sz, type_ref, index_ref, temps_ref, acc_ref, wall, xw, yw, emission):
    face = 1 - lax.axis_index("vert") % 2
    column = sub()
    kind = jnp.zeros_like(column)
    entry = jnp.zeros_like(column)
    for x in range(SUB):
        kind = jnp.where(column == x, type_ref[face, x], kind)
        entry = jnp.where(column == x, index_ref[face, x], entry)
    percent = jnp.zeros_like(column)
    for t in range(NTYPE):
        percent = jnp.where(kind == t, acc_ref[t], percent)
    alpha = percent.astype(jnp.float32) / 100.0
    heat = jnp.ones((SUB, LANES), jnp.float32)
    denom = jnp.ones((SUB, LANES), jnp.float32)

    def grid(number):
        index = lax.broadcasted_iota(jnp.int32, (1, -(-number // LANES) * LANES), 1)
        return node_speed(index, number), index < number

    vx, in_x = grid(sz.nx)
    vy, in_y = grid(sz.nv)
    for t in range(NTEMP):
        temp = jnp.full((1, 1), temps_ref[t], jnp.float32)
        along = jnp.sum(jnp.where(in_x, jnp.exp(-vx * vx / temp), 0.0), axis=1, keepdims=True)
        across = jnp.sum(
            jnp.where(in_y, jnp.maximum(vy, 0.0) * jnp.exp(-vy * vy / temp), 0.0),
            axis=1,
            keepdims=True,
        )
        inward = sz.weight * along * across / (math.pi * temp)
        heat = jnp.where(entry == t, temp, heat)
        denom = jnp.where(entry == t, inward, denom)
    wall[0] = 1.0 - alpha
    emitted = alpha / (denom * (math.pi * heat))
    vert_index = lax.axis_index("vert")
    inv_heat = 1.0 / heat
    wall_y = []
    for kg in range(sz.kg):
        vy = y_speed(sz, vert_index, kg)
        for r, value in enumerate((vy,) + beam_weights(vy)):
            yw[4 * kg + r] = value
        wall_y.append(masked(inside(sz, kg), emitted * jnp.exp(-vy * vy * inv_heat)))
    for xg in range(sz.xg):
        vx = x_speed(sz, xg)
        for r, value in enumerate((vx,) + beam_weights(vx)):
            xw[4 * xg + r] = value
        wall_x = jnp.exp(-vx * vx * inv_heat)
        for kg in range(sz.kg):
            diffuse = wall_x * wall_y[kg]
            emission[xg * sz.kg + kg] = diffuse
            emission[sz.tiles + xg * sz.kg + kg] = 0.5 * heat * diffuse


def chunk_copy(sz, source, target, sems, f, kg):
    rows = pl.ds(kg * PART_K, min(PART_K, sz.band - kg * PART_K))
    return pltpu.make_async_copy(
        source.at[f, rows], target.at[f, rows], sems.at[f * sz.kg + kg]
    )


def first_kernel(sz, argument, state, mirror, packet, right, left, sums_ref, turn, given, sems):
    vert_index = lax.axis_index("vert")
    parity = vert_index % 2
    for f in range(2):
        for kg in range(sz.kg):
            chunk_copy(sz, argument, given, sems, f, kg).start()
    for f in range(2):
        for kg in range(sz.kg):
            chunk_copy(sz, argument, given, sems, f, kg).wait()
            for xg in range(sz.xg):
                parts = []
                for k in range(kg * PART_K, (kg + 1) * PART_K):
                    if k < sz.band:
                        parts.append(given[f, k, xg * PART_X : (xg + 1) * PART_X, :])
                    else:
                        parts.append(jnp.zeros((PART_X, sz.cells), jnp.float32))
                turned = jnp.concatenate(parts, axis=0).T
                t = xg * sz.kg + kg
                slot = xg % 6
                for x in range(SUB):
                    for part in range(0, Y, SUB):
                        piece = turned[x * Y + part : x * Y + part + SUB, :]
                        turn[slot, pl.ds(part * SUB + x, SUB, stride=SUB), :] = piece
                base = sz.base(f, t)
                for step in range(Y):
                    y = real_row(parity, step)
                    state[pl.ds(base + step * SUB, SUB), :] = turn[slot, block(y * SUB), :]

    def step_body(step, carry):
        totals = None
        for xg in range(sz.xg):
            sums = None
            for kg in range(sz.kg):
                g, h = [state[block(sz.base(f, xg * sz.kg + kg) + step * SUB), :] for f in range(2)]
                sums = add_columns(y_speed(sz, vert_index, kg), g, h, sums)
            totals = add_group(x_speed(sz, xg), sums, totals)
        put_sums(sums_ref, real_row(parity, step), totals)
        return carry

    lax.fori_loop(0, Y, step_body, 0)
    send(sz, vert_index, state, sums_ref, mirror, packet, right, left)


def fields_of(parity, tot):
    def row(r):
        return tot[r // SUB][r % SUB : r % SUB + 1, :]

    n, mx, my, energy, pxx, pxy, pyy, tx, ty = [row(r) for r in range(9)]
    inv_n = 1.0 / n
    ux, uy = mx * inv_n, my * inv_n
    usq = ux * ux + uy * uy
    theta = 2.0 / 3.0 * (energy * inv_n - usq)
    along = ux * mx + uy * my
    qx = tx - 2.0 * (ux * pxx + uy * pxy) + usq * mx - ux * energy + 2.0 * ux * along - ux * usq * n
    qy = ty - 2.0 * (ux * pxy + uy * pyy) + usq * my - uy * energy + 2.0 * uy * along - uy * usq * n
    inv_t = 1.0 / theta
    rate = (time_increment * relaxation_multiplier) * n * jnp.exp(shear_exponent * jnp.log(theta))
    amount = rate * n * inv_t * (1.0 / math.pi)
    scale = (1.0 - diffusivity_ratio) * 0.8 * inv_n * inv_t * inv_t
    flux = jnp.where(parity == 0, row(10), row(9))
    return [ux, uy, inv_t, amount, scale * qx, scale * qy, 0.5 * theta, rate, flux]


def advect_kernel(sz, state, xw, yw, out):
    column = sub()

    def advance(step, near_at, far_at):
        for xg in range(sz.xg):
            x0 = 1.0 + xw[4 * xg + 1]
            x1, x2 = xw[4 * xg + 2], xw[4 * xg + 3]
            for kg in range(sz.kg):
                t = xg * sz.kg + kg
                c0 = x0 + yw[4 * kg + 1]
                y1, y2 = yw[4 * kg + 2], yw[4 * kg + 3]
                for f in range(2):
                    at = sz.base(f, t) + step * SUB
                    v = state[block(at), :]
                    if t >= sz.half:
                        one = jnp.where(column < 1, 0.0, state[pl.ds(at - 1, SUB), :])
                        two = jnp.where(column < 2, 0.0, state[pl.ds(at - 2, SUB), :])
                    else:
                        one = jnp.where(column >= SUB - 1, 0.0, state[pl.ds(at + 1, SUB), :])
                        two = jnp.where(column >= SUB - 2, 0.0, state[pl.ds(at + 2, SUB), :])
                    moved = v * c0 + (x1 * one + x2 * two)
                    if near_at:
                        moved = moved + y1 * state[block(at - SUB), :]
                    if far_at:
                        moved = moved + y2 * state[block(at - 2 * SUB), :]
                    out[block(at), :] = moved

    advance(0, False, False)
    advance(1, True, False)

    def body(step, carry):
        advance(step, True, True)
        return carry

    lax.fori_loop(2, Y, body, 0)


def spread_fields(sz, rows, spread):
    index = lax.broadcasted_iota(jnp.int32, (ROWS, LANES), 0)
    table = jnp.zeros((ROWS, sz.cells), jnp.float32)
    for r, value in enumerate(rows):
        table = jnp.where(index == r, value, table)
    parts = []
    for _ in range(3):
        part = table.astype(jnp.bfloat16)
        parts.append(part)
        table = table - part.astype(jnp.float32)
    parts = jnp.concatenate(parts, axis=0)
    index = lax.broadcasted_iota(jnp.int32, (3 * ROWS, LANES), 0) % ROWS
    picks = [(index == r).astype(jnp.float32).astype(jnp.bfloat16) for r in range(FIELDS)]
    wide = lax.dot_general(
        parts, jnp.concatenate(picks, axis=1), (((0,), (0,)), ((), ())),
        preferred_element_type=jnp.float32,
    )
    for r in range(FIELDS):
        spread[r] = wide[:, r * LANES : (r + 1) * LANES]


def step_kernel(sz, last, *refs):
    refs = list(refs)
    state, inner, mirror_in, right_in, left_in, packet_in, wall, xw, yw, emission = refs[:10]
    others = refs[10 : 10 + sz.vert - 2]
    rest = refs[10 + sz.vert - 2 :]
    if last:
        (result, spread, out, turn, final, sems) = rest
    else:
        (out, mirror, packet, right, left, spread, sums_ref) = rest
    vert_index = lax.axis_index("vert")
    parity = vert_index % 2

    tot = [packet_in[SUB * b : SUB * b + SUB, :] + mirror_in[sz.mirror_blocks + b] for b in range(2)]
    for other in others:
        tot = [tot[b] + other[SUB * b : SUB * b + SUB, :] for b in range(2)]
    spread_fields(sz, fields_of(parity, tot), spread)

    keep = wall[0]
    flux = spread[FIELDS - 1, block(real_row(parity, 0) * SUB), :]
    column = sub()

    def ghost(d, f, t):
        return keep * mirror_in[sz.mirror_index(d, f, t)] + flux * emission[f * sz.tiles + t]

    def advance(step, beyond):
        y = real_row(parity, step)
        ux, uy, inv_t, amount, px, py, half_theta, rate = [
            spread[r, block(y * SUB), :] for r in range(FIELDS - 1)
        ]
        along_y = []
        for kg in range(sz.kg):
            cy = yw[4 * kg] - uy
            cy_sq = cy * cy * inv_t
            along_y.append((masked(inside(sz, kg), amount * jnp.exp(-cy_sq)), py * cy, cy_sq - 2.0))
        totals = None
        for xg in range(sz.xg):
            vx = xw[4 * xg]
            cx = vx - ux
            cx_sq = cx * cx * inv_t
            ex = jnp.exp(-cx_sq)
            pxs = px * cx
            sums = None
            for kg in range(sz.kg):
                t = xg * sz.kg + kg
                ey, pys, cys = along_y[kg]
                maxwell = ex * ey
                p = pxs + pys
                sg = maxwell * (1.0 + p * (cx_sq + cys))
                sh = half_theta * (sg + p * maxwell)
                values = []
                for f, source in ((0, sg), (1, sh)):
                    at = sz.base(f, t) + step * SUB
                    side = sz.side_base(f, t) + 2 * step
                    if t >= sz.half:
                        edge = jnp.where(column < 2, right_in[pl.ds(side, SUB), :], 0.0)
                    else:
                        start = side - (SUB - 2)
                        edge = jnp.where(column >= SUB - 2, left_in[pl.ds(start, SUB), :], 0.0)
                    moved = (inner[block(at), :] + edge) + (source - rate * state[block(at), :])
                    if beyond is not None:
                        moved = moved + beyond(f, t, yw[4 * kg + 2], yw[4 * kg + 3])
                    out[block(at), :] = moved
                    values.append(moved)
                if not last:
                    sums = add_columns(yw[4 * kg], values[0], values[1], sums)
            if not last:
                totals = add_group(vx, sums, totals)
        if not last:
            put_sums(sums_ref, y, totals)

    advance(0, lambda f, t, y1, y2: y1 * ghost(0, f, t) + y2 * ghost(1, f, t))
    advance(1, lambda f, t, y1, y2: y2 * ghost(0, f, t))

    def body(step, carry):
        advance(step, None)
        return carry

    lax.fori_loop(2, Y, body, 0)
    if not last:
        send(sz, vert_index, out, sums_ref, mirror, packet, right, left)
        return
    for f in range(2):
        for kg in range(sz.kg):
            for xg in range(sz.xg):
                t = xg * sz.kg + kg
                slot = xg % 6
                base = sz.base(f, t)
                for step in range(Y):
                    y = real_row(parity, step)
                    turn[slot, block(y * SUB), :] = out[pl.ds(base + step * SUB, SUB), :]
                parts = []
                for x in range(SUB):
                    for part in range(0, Y, SUB):
                        parts.append(turn[slot, pl.ds(part * SUB + x, SUB, stride=SUB), :])
                turned = jnp.concatenate(parts, axis=0).T
                for k in range(kg * PART_K, min((kg + 1) * PART_K, sz.band)):
                    row = (k - kg * PART_K) * PART_X
                    final[f, k, xg * PART_X : (xg + 1) * PART_X, :] = turned[row : row + PART_X, :]
            chunk_copy(sz, final, result, sems, f, kg).start()
    for f in range(2):
        for kg in range(sz.kg):
            chunk_copy(sz, final, result, sems, f, kg).wait()


def shapes(sz):
    f32 = jnp.float32
    side = jax.ShapeDtypeStruct((sz.side_rows, LANES), f32)
    return (
        jax.ShapeDtypeStruct((sz.state_rows, LANES), f32),
        jax.ShapeDtypeStruct((sz.mirror_blocks + 2, SUB, LANES), f32),
        jax.ShapeDtypeStruct((ROWS, sz.cells), f32),
        side,
        side,
    )


def on_device(distribution, wall_type, wall_temp_index, wall_temps, accommodation):
    _, band, nx, cells = distribution.shape
    vert = lax.axis_size("vert")
    columns = lax.axis_size("gx")
    sz = Sizes(band, nx, cells, vert)
    vmem = pl.BlockSpec(memory_space=pltpu.VMEM)
    smem = pl.BlockSpec(memory_space=pltpu.SMEM)
    hbm = pl.BlockSpec(memory_space=pltpu.HBM)
    final_shape = jax.ShapeDtypeStruct(distribution.shape, jnp.float32)
    bytes_moved = 2 * distribution.size * 4
    sums_scratch = pltpu.VMEM((FIELDS, sz.cells, LANES), jnp.float32)
    turn_scratch = pltpu.VMEM((6, sz.cells, LANES), jnp.float32)
    step_scratch = [pltpu.VMEM((FIELDS, sz.cells, LANES), jnp.float32)]
    first_vmem = ALL_VMEM - 26 * distribution.size
    stage = [
        pltpu.VMEM(distribution.shape, jnp.float32),
        pltpu.SemaphoreType.DMA((2 * sz.kg,)),
    ]
    state, mirror, packet, right, left = pl.pallas_call(
        functools.partial(first_kernel, sz),
        out_shape=shapes(sz),
        in_specs=[hbm],
        out_specs=(vmem,) * 5,
        scratch_shapes=[sums_scratch, turn_scratch] + stage,
        cost_estimate=pl.CostEstimate(
            flops=10 * distribution.size, bytes_accessed=bytes_moved, transcendentals=0
        ),
        compiler_params=pltpu.CompilerParams(vmem_limit_bytes=first_vmem),
        name="first",
    )(distribution)
    tables = pl.pallas_call(
        functools.partial(wall_kernel, sz),
        out_shape=tuple(
            jax.ShapeDtypeStruct((count, SUB, LANES), jnp.float32)
            for count in (1, 4 * sz.xg, 4 * sz.kg, 2 * sz.tiles)
        ),
        in_specs=[smem] * 4,
        out_specs=(vmem,) * 4,
        compiler_params=pltpu.CompilerParams(vmem_limit_bytes=KERNEL_VMEM),
        name="walls",
    )(wall_type, wall_temp_index, wall_temps, accommodation)
    ring = [(i, (i + 1) % columns) for i in range(columns)]
    back = [(j, i) for i, j in ring]
    for iteration in range(ITERS):
        last = iteration == ITERS - 1
        mirror_in = lax.ppermute(mirror, "vert", [(s, s ^ 1) for s in range(vert)])
        right_in = lax.ppermute(right, "gx", ring)
        left_in = lax.ppermute(left, "gx", back)
        others = []
        for mask in range(vert - 1, 1, -1):
            others.append(lax.ppermute(packet, "vert", [(s, s ^ mask) for s in range(vert)]))
        inner = pl.pallas_call(
            functools.partial(advect_kernel, sz),
            out_shape=jax.ShapeDtypeStruct((sz.state_rows, LANES), jnp.float32),
            in_specs=[vmem] * 3,
            out_specs=vmem,
            cost_estimate=pl.CostEstimate(
                flops=12 * distribution.size, bytes_accessed=bytes_moved, transcendentals=0
            ),
            compiler_params=pltpu.CompilerParams(vmem_limit_bytes=KERNEL_VMEM),
            name="advect",
        )(state, tables[1], tables[2])
        if last:
            scratch = step_scratch + [pltpu.VMEM((sz.state_rows, LANES), jnp.float32), turn_scratch] + stage
        else:
            scratch = step_scratch + [sums_scratch]
        result = pl.pallas_call(
            functools.partial(step_kernel, sz, last),
            out_shape=(final_shape,) if last else shapes(sz),
            in_specs=[vmem] * (10 + len(others)),
            out_specs=(hbm,) if last else (vmem,) * 5,
            scratch_shapes=scratch,
            cost_estimate=pl.CostEstimate(
                flops=40 * distribution.size, bytes_accessed=bytes_moved, transcendentals=0
            ),
            compiler_params=pltpu.CompilerParams(vmem_limit_bytes=KERNEL_VMEM),
            name="last" if last else "step",
        )(state, inner, mirror_in, right_in, left_in, packet, *tables, *others)
        if last:
            (state,) = result
        else:
            state, mirror, packet, right, left = result
    return state


def solution(mesh):
    placed = (P(None, "vert", None, "gx"), P(None, "gx"), P(None, "gx"), P(), P())
    return jax.shard_map(
        on_device,
        mesh=mesh,
        in_specs=placed,
        out_specs=P(None, "vert", None, "gx"),
        check_vma=False,
    )
```
